32 devices in a mesh: groups: 2 (over y), ctx: 4 (over z), head: 2 (over x), dp: 2 (over core).
Axes of the slice: x: 2, y: 2, z: 4, core: 2. Of those that a mesh axis runs over, the one named last changes fastest.
Arguments:
- queries: bfloat16 [4, 4, 512, 16, 128], P(('groups', 'dp'), 'ctx', None, 'head'), parts along dimension 0, may hold values from -6 to 6
- key_vecs: bfloat16 [4, 4, 512, 16, 128], P(('groups', 'dp'), 'ctx', None, 'head'), parts along dimension 0, may hold values from -6 to 6
- value_vecs: bfloat16 [4, 4, 512, 16, 128], P(('groups', 'dp'), 'ctx', None, 'head'), parts along dimension 0, may hold values from -6 to 6
- grad_out: bfloat16 [4, 4, 512, 16, 128], P(('groups', 'dp'), 'ctx', None, 'head'), parts along dimension 0, may hold values from -6 to 6
Outputs:
- attended: bfloat16 [4, 4, 512, 16, 128], P(('groups', 'dp'), 'ctx', None, 'head'), parts along dimension 0
- grad_queries: bfloat16 [4, 4, 512, 16, 128], P(('groups', 'dp'), 'ctx', None, 'head'), parts along dimension 0
- grad_keys: bfloat16 [4, 4, 512, 16, 128], P(('groups', 'dp'), 'ctx', None, 'head'), parts along dimension 0
- grad_values: bfloat16 [4, 4, 512, 16, 128], P(('groups', 'dp'), 'ctx', None, 'head'), parts along dimension 0
The draws below stay inside these ranges and needn't reach their ends.
There are 2 independent parts, one for each index of `groups`. The reference program is written for one: setup_inputs(seed, part) draws one part's arguments, and reference() takes and returns one part's arrays. A program takes and returns all parts, laid end to end along the dimension named above; each array names one. Nothing has to cross between parts.
All inputs are finite; a program needn't handle non-finite values.
Results may differ from the reference program's by a relative error of at most 0.013.
Values may be sent and summed in bfloat16 or wider, within the bound.
A program may use at most 128 MiB of HBM per device.

```python
import math
import jax
import jax.numpy as jnp
from jax import lax

HEADS = 16
HEAD_DIM = 128
COLS = 512
ROWS = 4
BATCH = 2


def draw_queries(key, part):
    shape = (BATCH, ROWS, COLS, HEADS, HEAD_DIM)
    values = jnp.clip(jax.random.normal(jax.random.fold_in(key, 11), shape, jnp.float32), -6.0, 6.0)
    return values.astype(jnp.bfloat16)


def draw_key_vecs(key, part):
    shape = (BATCH, ROWS, COLS, HEADS, HEAD_DIM)
    values = jnp.clip(jax.random.normal(jax.random.fold_in(key, 21), shape, jnp.float32), -6.0, 6.0)
    return values.astype(jnp.bfloat16)


def shard_levels(stream_key, shape, cuts, least, high):
    factor_of = 1.0
    for axis_at, parts in cuts:
        draws = jax.random.uniform(jax.random.fold_in(jax.random.fold_in(stream_key, 6), axis_at), (parts,), jnp.float32, least / len(cuts), high / len(cuts))
        factor_of = factor_of * jnp.repeat(jnp.exp(draws), shape[axis_at] // parts).reshape((-1,) + (1,) * (len(shape) - 1 - axis_at))
    return factor_of


def centred(rng, shape, width, limit, cuts=(), kind=jnp.bfloat16):
    drawn = width * jax.random.normal(rng, shape, jnp.float32)
    if cuts:
        drawn = drawn * shard_levels(rng, shape, cuts, -0.22, 0.18)
    return jnp.clip(drawn, -limit, limit).astype(kind)


def setup_inputs(seed: int = 0, part: int = 0) -> dict:
    seeds = jax.random.split(jax.random.key(seed), 5)
    part_keys = jax.random.split(jax.random.fold_in(seeds[4], part), 5)
    return {
        "queries": draw_queries(jax.random.fold_in(jax.random.fold_in(seeds[4], part), 71), part),
        "key_vecs": draw_key_vecs(jax.random.fold_in(jax.random.fold_in(seeds[4], part), 71), part),
        "value_vecs": centred(part_keys[2], (BATCH, ROWS, COLS, HEADS, HEAD_DIM), 1.0, 6.0, ((0, 2), (1, 4), (3, 2))),
        "grad_out": centred(part_keys[3], (BATCH, ROWS, COLS, HEADS, HEAD_DIM), 1.0, 6.0, ((0, 2), (1, 4), (3, 2))),
    }


def causal(length):
    positions = jnp.arange(length)
    return positions[None, :] <= positions[:, None]

def attend(query_in, key_in, value_in, grad_in, layout, allowed):
    scaling = 1.0 / math.sqrt(HEAD_DIM)
    key_form = layout.replace('q', 'k')
    query_f = query_in.astype(jnp.float32)
    key_f = key_in.astype(jnp.float32)
    value_f = value_in.astype(jnp.float32)
    grad_f = grad_in.astype(jnp.float32)
    scores = jnp.einsum(layout + ',' + key_form + '->bxhqk', query_f, key_f) * scaling
    scores = jnp.where(allowed, scores, -1e+30)
    highest = lax.optimization_barrier(jnp.max(scores, axis=-1, keepdims=True))
    weight_sum = lax.optimization_barrier(jnp.sum(jnp.exp(scores - highest), axis=-1, keepdims=True))
    log_total = highest + jnp.log(weight_sum)
    weights = jnp.where(allowed, jnp.exp(scores - log_total), 0.0)
    rounded = lax.optimization_barrier(weights.astype(jnp.bfloat16)).astype(jnp.float32)
    output = jnp.einsum('bxhqk,' + key_form + '->' + layout, rounded, value_f).astype(jnp.bfloat16)
    output_f = lax.optimization_barrier(output).astype(jnp.float32)
    row_dots = jnp.einsum(layout + ',' + layout + '->bxhq', grad_f, output_f)
    dprobs = jnp.einsum(layout + ',' + key_form + '->bxhqk', grad_f, value_f)
    dscores = (weights * (dprobs - row_dots[..., None]) * scaling).astype(jnp.bfloat16)
    dscores = lax.optimization_barrier(dscores).astype(jnp.float32)
    grad_query = jnp.einsum('bxhqk,' + key_form + '->' + layout, dscores, key_f).astype(jnp.bfloat16)
    grad_key = jnp.einsum('bxhqk,' + layout + '->' + key_form, dscores, query_f).astype(jnp.bfloat16)
    grad_value = jnp.einsum('bxhqk,' + layout + '->' + key_form, rounded, grad_f).astype(jnp.bfloat16)
    return (output, grad_query, grad_key, grad_value)

def merge_heads(first_part, second_part):
    stacked = jnp.stack((first_part, second_part), axis=4)
    shape = first_part.shape
    return stacked.reshape(shape[:3] + (2 * shape[3], shape[4]))

def row_block(pieces):
    widened = tuple((piece[:, None] for piece in pieces))
    results = attend(widened[0], widened[1], widened[2], widened[3], 'bxqhd', causal(COLS))
    return tuple((result[:, 0] for result in results))

def reference(queries, key_vecs, value_vecs, grad_out):
    arrays = (queries, key_vecs, value_vecs, grad_out)
    row_parts = tuple((jnp.moveaxis(array[:, :, :, 0::2], 1, 0) for array in arrays))
    col_parts = tuple((array[:, :, :, 1::2] for array in arrays))
    row_results = lax.map(row_block, row_parts)
    row_results = tuple((jnp.moveaxis(result, 0, 1) for result in row_results))
    col_results = attend(col_parts[0], col_parts[1], col_parts[2], col_parts[3], 'bqxhd', causal(ROWS))
    return (merge_heads(row_results[0], col_results[0]), merge_heads(row_results[1], col_results[1]), merge_heads(row_results[2], col_results[2]), merge_heads(row_results[3], col_results[3]))
```

```python
import functools
import math

import jax
import jax.numpy as jnp
from jax import lax
from jax.experimental import pallas as pl
from jax.experimental.pallas import tpu as pltpu
from jax.sharding import PartitionSpec as P

MESH = pl.DeviceIdType.MESH
F32 = jnp.float32
BF16 = jnp.bfloat16
NT = (((1,), (1,)), ((), ()))
NN = (((1,), (0,)), ((), ()))
TN = (((0,), (0,)), ((), ()))


def mm(a, b, dims):
    return lax.dot_general(a, b, dims, preferred_element_type=F32)


def row_piece(buf, acc, stage, i, b, tokens, depth):
    scaling = 1.0 / math.sqrt(depth)
    block = tokens // 2
    rows = pl.ds(b * block, block)
    span = (b + 1) * block
    q = buf[i, Q, rows]
    g = buf[i, G, rows]
    k = buf[i, K, pl.ds(0, span)]
    v = buf[i, V, pl.ds(0, span)]
    s = mm(q, k, NT) * scaling
    qpos = lax.broadcasted_iota(jnp.int32, (block, span), 0) + b * block
    kpos = lax.broadcasted_iota(jnp.int32, (block, span), 1)
    s = jnp.where(kpos <= qpos, s, -1e30)
    top = jnp.max(s, axis=-1, keepdims=True)
    e = jnp.exp(s - top)
    p = e * (1.0 / jnp.sum(e, axis=-1, keepdims=True))
    pb = p.astype(BF16)
    o = mm(pb, v, NN).astype(BF16)
    dots = jnp.sum(g.astype(F32) * o.astype(F32), axis=-1, keepdims=True)
    dp = mm(g, v, NT)
    ds = (p * (dp - dots) * scaling).astype(BF16)
    stage[i, 0, rows] = o
    stage[i, 1, rows] = mm(ds, k, NN).astype(BF16)
    dk = mm(ds, q, TN)
    dv = mm(pb, g, TN)
    if b == 1:
        acc[0] = dk[:block]
        acc[1] = dv[:block]
        stage[i, 2, rows] = dk[block:].astype(BF16)
        stage[i, 3, rows] = dv[block:].astype(BF16)
    else:
        stage[i, 2, rows] = (acc[0] + dk).astype(BF16)
        stage[i, 3, rows] = (acc[1] + dv).astype(BF16)


def dot(a, b):
    return jnp.sum(a * b, axis=-1, keepdims=True)


def add_up(terms):
    return functools.reduce(jnp.add, terms)


def attend_to(q, g, keys, scaling, rest=None):
    s = [dot(q, k) * scaling for k, _ in keys]
    dp = [dot(g, v) for _, v in keys]
    if rest is not None:
        s, dp = s + [rest[0]], dp + [rest[1]]
    top = functools.reduce(jnp.maximum, s)
    e = [jnp.exp(x - top) for x in s]
    total = add_up(e)
    inverse = 1.0 / total
    p = [x * inverse for x in e]
    dots = add_up([x * y for x, y in zip(p, dp)])
    ds = [x * (y - dots) * scaling for x, y in zip(p, dp)]
    o = add_up([x * kv[1] for x, kv in zip(p, keys)])
    dq = add_up([x * kv[0] for x, kv in zip(ds, keys)])
    return o, dq, p, ds, top + jnp.log(total), dots


def to_rows(columns):
    tokens = columns[0].shape[0]
    lane = lax.broadcasted_iota(jnp.int32, (tokens, 128), 1)
    wide = jnp.broadcast_to(columns[0], (tokens, 128))
    for i, x in enumerate(columns[1:], 1):
        wide = jnp.where(lane == i, x, wide)
    return jnp.transpose(wide)[:8]


def stack_rows(rows):
    index = lax.broadcasted_iota(jnp.int32, (8, rows[0].shape[1]), 0)
    out = jnp.broadcast_to(rows[0], index.shape)
    for i, x in enumerate(rows[1:], 1):
        out = jnp.where(index == i, x, out)
    return out


def to_columns(rows, count):
    turned = jnp.transpose(jnp.concatenate([rows] * 16, axis=0))
    return [turned[:, i : i + 1] for i in range(count)]


Q, G, K, V = 0, 1, 2, 3
QUARTERS = 4
KV0, KV1, QG2, QG3, SC, GA, GB, OD_A, OD_B, SCD = range(10)


def each(first, last, body):
    def step(i, _):
        body(i)
        return 0

    lax.fori_loop(first, last, step, 0)


def kernel(
    q_ref, k_ref, v_ref, g_ref, o_out, dq_out, dk_out, dv_out,
    fetched, wide, rows_in, cols_in, rows_stage, cols_stage, acc, own_grads,
    kv0, kv1, qg2, qg3, sc, grads_a, grads_b, od_a, od_b, scd,
    sc_stage, scd_stage, send_a, send_b, send_c,
    load, sent, got,
):
    tokens, local_heads, depth = q_ref.shape
    heads = local_heads // 2
    columns = tokens // QUARTERS
    chunks = heads * QUARTERS
    scaling = 1.0 / math.sqrt(depth)
    me = lax.axis_index("ctx")
    refs = (q_ref, g_ref, k_ref, v_ref)
    outs = (o_out, dq_out, dk_out, dv_out)
    shift = jnp.where(me < 2, 1, 0)

    def turn(step):
        return lax.rem(step + shift, QUARTERS)

    def fetch(at, quarter):
        part = pl.ds(quarter * columns, columns)
        return pltpu.make_async_copy(refs[at].at[part], fetched.at[at, part], load.at[at, quarter])

    @pl.when(me < 2)
    def _():
        for step in range(QUARTERS):
            for at in (K, V, Q, G):
                fetch(at, turn(step)).start()

    @pl.when(me >= 2)
    def _():
        for step in range(QUARTERS):
            for at in (Q, G, K, V):
                fetch(at, turn(step)).start()

    barrier = pltpu.get_barrier_semaphore()

    def greet(target):
        pl.semaphore_signal(barrier, inc=1, device_id={"ctx": target}, device_id_type=MESH)

    @pl.when(me == 1)
    def _():
        greet(0)
        greet(2)

    @pl.when(me == 2)
    def _():
        greet(1)
        greet(3)

    def remote(src, dst, send, recv, c, target):
        return pltpu.make_async_remote_copy(
            src_ref=src, dst_ref=dst, send_sem=sent.at[send, c], recv_sem=got.at[recv, c],
            device_id={"ctx": target}, device_id_type=MESH,
        )

    def pair_of(c, first):
        return cols_in.at[c, pl.ds(first, 2)]

    def split(at, quarter):
        fetch(at, quarter).wait()
        x = fetched[at, pl.ds(quarter * columns, columns)].astype(F32)
        wide[at] = x.reshape(columns * local_heads, depth)
        for h in range(local_heads):
            x = wide[at, pl.ds(h, columns, stride=local_heads)].astype(BF16)
            if h % 2 == 0:
                rows_in[h // 2, at, pl.ds(quarter * columns, columns)] = x
            else:
                cols_in[quarter * heads + h // 2, at] = x

    def join(a, quarter):
        part = pl.ds(quarter * columns, columns)
        for h in range(local_heads):
            x = rows_stage[h // 2, a, part] if h % 2 == 0 else cols_stage[quarter * heads + h // 2, a]
            wide[a, pl.ds(h, columns, stride=local_heads)] = x.astype(F32)
        outs[a][part] = wide[a].reshape(columns, local_heads, depth).astype(BF16)

    def vectors(buf, c):
        return [buf[c, a].astype(F32) for a in range(buf.shape[1])]

    def put(ref, c, first, values):
        for a, x in enumerate(values):
            ref[c, first + a] = x.astype(ref.dtype)

    def kv0_copy(c):
        return remote(pair_of(c, K), kv0.at[c], 0, KV0, c, 1)

    def kv0_forward(c):
        return remote(kv0.at[c], kv0.at[c], 0, KV0, c, 2)

    def kv1_copy(c):
        return remote(pair_of(c, K), kv1.at[c], 1, KV1, c, 2)

    def grads_1_to_0(c):
        return remote(send_a.at[c], grads_b.at[c], 2, GB, c, 0)

    def od_1_to_2(c):
        return remote(send_b.at[c], od_b.at[c], 3, OD_B, c, 2)

    def od_1_to_3(c):
        return remote(send_c.at[c], od_b.at[c], 4, OD_B, c, 3)

    def scd_1_to(c, target):
        return remote(scd_stage.at[c], scd.at[c], 3 + target, SCD, c, target)

    def qg2_copy(c):
        return remote(pair_of(c, Q), qg2.at[c], 0, QG2, c, 1)

    def qg3_forward(c):
        return remote(qg3.at[c], qg3.at[c], 1, QG3, c, 1)

    def sc_2_to_1(c):
        return remote(sc_stage.at[1, c], sc.at[c], 2, SC, c, 1)

    def grads_2_to_0(c):
        return remote(send_a.at[c], grads_a.at[c], 3, GA, c, 0)

    def grads_2_to_1(c):
        return remote(send_b.at[c], grads_a.at[c], 4, GA, c, 1)

    def od_2_to_3(c):
        return remote(send_c.at[c], od_a.at[c], 5, OD_A, c, 3)

    def scd_2_to_3(c):
        return remote(scd_stage.at[c], scd.at[c], 6, SCD, c, 3)

    def qg3_copy(c):
        return remote(pair_of(c, Q), qg3.at[c], 0, QG3, c, 2)

    def sc_3_to_2(c):
        return remote(sc_stage.at[0, c], sc.at[c], 1, SC, c, 2)

    @pl.when(me == 0)
    def _():
        def go(step):
            quarter = turn(step)
            split(K, quarter)
            split(V, quarter)

            @pl.when(step == 0)
            def _():
                pl.semaphore_wait(barrier, 1)

            each(0, heads, lambda i: kv0_copy(quarter * heads + i).start())
            split(Q, quarter)
            split(G, quarter)

        each(0, QUARTERS, go)

    @pl.when(me == 1)
    def _():
        split(K, 1)
        split(V, 1)
        pl.semaphore_wait(barrier, 1)
        kv1_copy(heads).start()
        kv1_copy(heads + 1).start()

    @pl.when(me == 2)
    def _():
        split(Q, 0)
        split(G, 0)
        pl.semaphore_wait(barrier, 1)
        each(0, heads, lambda c: qg2_copy(c).start())
        split(K, 0)
        split(V, 0)

        def go(c):
            qg3_copy(c).wait_recv()
            qg3_forward(c).start()
            q, g, k, v = vectors(cols_in, c)
            q3, g3 = vectors(qg3, c)
            own = to_rows([dot(q, k) * scaling, dot(g, v), dot(q3, k) * scaling, dot(g3, v)])
            sc_stage[0, c] = own
            sc_3_to_2(c).wait_recv()
            far = sc[c]
            s32, dp32, s33, dp33 = own[2:3], own[3:4], far[0:1], far[1:2]
            top = jnp.maximum(s32, s33)
            e32, e33 = jnp.exp(s32 - top), jnp.exp(s33 - top)
            total = e32 + e33
            mean = (e32 * dp32 + e33 * dp33) / total
            sc_stage[1, c] = stack_rows([own[0:1], own[1:2], top + jnp.log(total), mean])
            sc_2_to_1(c).start()

            @pl.when(c < QUARTERS - 1)
            def _():
                for at in range(4):
                    split(at, c + 1)

        each(0, heads, go)

    @pl.when(me == 3)
    def _():
        def go(quarter):
            split(Q, quarter)
            split(G, quarter)

            @pl.when(quarter == 0)
            def _():
                pl.semaphore_wait(barrier, 1)

            each(0, heads, lambda i: qg3_copy(quarter * heads + i).start())
            split(K, quarter)
            split(V, quarter)

            def scores(i):
                c = quarter * heads + i
                q, g, k, v = vectors(cols_in, c)
                sc_stage[0, c] = to_rows([dot(q, k) * scaling, dot(g, v)])
                sc_3_to_2(c).start()

            each(0, heads, scores)

        each(0, QUARTERS, go)

    def chunk_0(t):
        c = jnp.where(t < 2 * heads, t + heads, jnp.where(t < 3 * heads, t - 2 * heads, t))
        q, g, k, v = vectors(cols_in, c)
        o, dq, p, ds, _, _ = attend_to(q, g, [(k, v)], scaling)
        put(cols_stage, c, 0, (o, dq))
        grads_1_to_0(c).wait_recv()
        near = vectors(grads_b, c)
        total = (ds[0] * q + near[0], p[0] * g + near[1])

        @pl.when(c < heads)
        def _():
            put(cols_stage, c, 2, total)

        @pl.when(c >= heads)
        def _():
            grads_2_to_0(c).wait_recv()
            far = vectors(grads_a, c)
            put(cols_stage, c, 2, (total[0] + far[0], total[1] + far[1]))

    def chunk_1a(t):
        c = t + heads
        kv0_copy(c).wait_recv()
        kv0_forward(c).start()

        @pl.when((t % 2 == 1) & (t <= 5))
        def _():
            split(K, (t // 2 + 2) % QUARTERS)
            split(V, (t // 2 + 2) % QUARTERS)

        @pl.when(c + 2 < chunks)
        def _():
            kv1_copy(c + 2).start()

        @pl.when((t % 2 == 0) & (t <= 6))
        def _():
            split(Q, (t // 2 + 1) % QUARTERS)
            split(G, (t // 2 + 1) % QUARTERS)

        q, g, k, v = vectors(cols_in, c)
        k0, v0 = vectors(kv0, c)
        o, dq, p, ds, _, _ = attend_to(q, g, [(k0, v0), (k, v)], scaling)
        put(send_a, c, 0, (ds[0] * q, p[0] * g))
        grads_1_to_0(c).start()
        put(cols_stage, c, 0, (o, dq))
        put(own_grads, c, 0, (ds[1] * q, p[1] * g))

    def chunk_1b(c):
        kv0_copy(c).wait_recv()
        qg2_copy(c).wait_recv()
        qg3_copy(c).wait_recv()
        sc_2_to_1(c).wait_recv()
        q, g, k, v = vectors(cols_in, c)
        k0, v0 = vectors(kv0, c)
        keys = [(k0, v0), (k, v)]
        rest = to_columns(sc[c], 4)
        q2, g2 = vectors(qg2, c)
        o2, dq2, p2, ds2, lse2, dots2 = attend_to(q2, g2, keys, scaling, rest[:2])
        q3, g3 = vectors(qg3, c)
        o3, dq3, p3, ds3, lse3, dots3 = attend_to(q3, g3, keys, scaling, rest[2:])
        scd_stage[c] = to_rows([lse3, dots3, lse2, dots2])
        scd_1_to(c, 2).start()
        scd_1_to(c, 3).start()
        put(send_b, c, 0, (o2, dq2))
        od_1_to_2(c).start()
        put(send_c, c, 0, (o3, dq3))
        od_1_to_3(c).start()
        o, dq, p, ds, _, _ = attend_to(q, g, keys, scaling)
        put(cols_stage, c, 0, (o, dq))
        dk = [ds[j] * q + ds2[j] * q2 + ds3[j] * q3 for j in range(2)]
        dv = [p[j] * g + p2[j] * g2 + p3[j] * g3 for j in range(2)]
        put(send_a, c, 0, (dk[0], dv[0]))
        grads_1_to_0(c).start()
        put(cols_stage, c, 2, (dk[1], dv[1]))

    def chunk_2a(t):
        c = t + heads
        kv1_copy(c).wait_recv()
        kv0_forward(c).wait_recv()
        qg3_copy(c).wait_recv()
        sc_3_to_2(c).wait_recv()
        q, g, k, v = vectors(cols_in, c)
        q3, g3 = vectors(qg3, c)
        k0, v0 = vectors(kv0, c)
        k1, v1 = vectors(kv1, c)
        keys = [(k0, v0), (k1, v1), (k, v)]
        rest = to_columns(sc[c], 2)
        o, dq, p, ds, _, _ = attend_to(q, g, keys, scaling)
        o3, dq3, p3, ds3, lse3, dots3 = attend_to(q3, g3, keys, scaling, rest)
        dk = [ds[j] * q + ds3[j] * q3 for j in range(3)]
        dv = [p[j] * g + p3[j] * g3 for j in range(3)]
        put(send_a, c, 0, (dk[0], dv[0]))
        grads_2_to_0(c).start()
        put(send_b, c, 0, (dk[1], dv[1]))

        @pl.when(t >= LAG)
        def _():
            grads_2_to_1(c - LAG).start()

        @pl.when(t == 3 * heads - 1)
        def _():
            for late in range(LAG):
                grads_2_to_1(chunks - LAG + late).start()

        scd_stage[c] = to_rows([lse3, dots3])
        scd_2_to_3(c).start()
        put(send_c, c, 0, (o3, dq3))
        od_2_to_3(c).start()
        put(cols_stage, c, 0, (o, dq, dk[2], dv[2]))

    def chunk_2b(c):
        scd_1_to(c, 2).wait_recv()
        own, far = sc_stage[0, c], scd[c]
        p3 = jnp.exp(own[2:3] - far[0:1])
        ds3 = p3 * (own[3:4] - far[1:2]) * scaling
        p2 = jnp.exp(own[0:1] - far[2:3])
        ds2 = p2 * (own[1:2] - far[3:4]) * scaling
        p3, ds3, p2, ds2 = to_columns(stack_rows([p3, ds3, p2, ds2]), 4)
        q, g, k, v = vectors(cols_in, c)
        put(send_c, c, 0, (p3 * v, ds3 * k))
        od_2_to_3(c).start()
        q3, g3 = vectors(qg3, c)
        put(cols_stage, c, 2, (ds2 * q + ds3 * q3, p2 * g + p3 * g3))
        od_1_to_2(c).wait_recv()
        far = vectors(od_b, c)
        put(cols_stage, c, 0, (p2 * v + far[0], ds2 * k + far[1]))

    def chunk_3(c):
        @pl.when(c < heads)
        def _():
            scd_1_to(c, 3).wait_recv()

        @pl.when(c >= heads)
        def _():
            scd_2_to_3(c).wait_recv()

        own, far = sc_stage[0, c], scd[c]
        p = jnp.exp(own[0:1] - far[0:1])
        ds = p * (own[1:2] - far[1:2]) * scaling
        p, ds = to_columns(stack_rows([p, ds]), 2)
        q, g, k, v = vectors(cols_in, c)
        put(cols_stage, c, 2, (ds * q, p * g))
        od_2_to_3(c).wait_recv()
        near = vectors(od_a, c)
        total = (p * v + near[0], ds * k + near[1])

        @pl.when(c >= heads)
        def _():
            put(cols_stage, c, 0, total)

        @pl.when(c < heads)
        def _():
            od_1_to_3(c).wait_recv()
            far = vectors(od_b, c)
            put(cols_stage, c, 0, (total[0] + far[0], total[1] + far[1]))

    first_row = jnp.where(me == 1, 7, 1)

    def body(t):
        piece = t - first_row
        here = (piece >= 0) & (piece < 2 * heads)

        @pl.when(here & (piece % 2 == 0))
        def _():
            row_piece(rows_in, acc, rows_stage, piece // 2, 1, tokens, depth)

        @pl.when(here & (piece % 2 == 1))
        def _():
            row_piece(rows_in, acc, rows_stage, piece // 2, 0, tokens, depth)

        @pl.when((me != 1) & ((t == 2 * heads + 1) | (t == 2 * heads + 2) | (t == 3 * heads)))
        def _():
            third = jnp.where(me == 0, 0, 3)
            for a in range(4):
                join(a, jnp.where(t == 3 * heads, third, t - 2 * heads))

        @pl.when(me == 0)
        def _():
            chunk_0(t)

        @pl.when((me == 1) & (t < 3 * heads))
        def _():
            chunk_1a(t)

        @pl.when((me == 1) & (t >= 3 * heads))
        def _():
            chunk_1b(t - 3 * heads)

        @pl.when((me == 2) & (t < 3 * heads))
        def _():
            chunk_2a(t)

        @pl.when((me == 2) & (t >= 3 * heads))
        def _():
            chunk_2b(t - 3 * heads)

        @pl.when(me == 3)
        def _():
            chunk_3((t + heads) % chunks)

    each(0, chunks, body)
    last = jnp.where(me == 0, 3, 0)
    for a in range(4):
        join(a, last)

    @pl.when(me == 1)
    def _():
        def join_early(quarter):
            join(0, quarter)
            join(1, quarter)

        each(1, QUARTERS, join_early)

        def finish(c):
            grads_2_to_1(c).wait_recv()
            far = vectors(grads_a, c)
            put(cols_stage, c, 2, [own_grads[c, a] + far[a] for a in range(2)])

            @pl.when(c % heads == heads - 1)
            def _():
                join(2, c // heads)
                join(3, c // heads)

        each(heads, chunks, finish)

    @pl.when(me == 0)
    def _():
        each(0, chunks, lambda c: kv0_copy(c).wait_send())

    @pl.when(me == 1)
    def _():
        def done(c):
            kv0_forward(c).wait_send()
            kv1_copy(c).wait_send()

        each(heads, chunks, done)
        each(0, chunks, lambda c: grads_1_to_0(c).wait_send())

        def done_b(c):
            od_1_to_2(c).wait_send()
            od_1_to_3(c).wait_send()
            scd_1_to(c, 2).wait_send()
            scd_1_to(c, 3).wait_send()

        each(0, heads, done_b)

    @pl.when(me == 2)
    def _():
        def done_b(c):
            qg2_copy(c).wait_send()
            qg3_forward(c).wait_send()
            sc_2_to_1(c).wait_send()

        each(0, heads, done_b)

        def done(c):
            grads_2_to_0(c).wait_send()
            grads_2_to_1(c).wait_send()
            scd_2_to_3(c).wait_send()

        each(heads, chunks, done)
        each(0, chunks, lambda c: od_2_to_3(c).wait_send())

    @pl.when(me == 3)
    def _():
        def done(c):
            qg3_copy(c).wait_send()
            sc_3_to_2(c).wait_send()

        each(0, chunks, done)


LAG = 2


def store_kernel(*refs):
    ins, outs, leave = refs[:4], refs[4:8], refs[8]
    copies = [pltpu.make_async_copy(x, y, leave.at[a]) for a, (x, y) in enumerate(zip(ins, outs))]
    for copy in copies:
        copy.start()
    for copy in copies:
        copy.wait()


def fused(queries, key_vecs, value_vecs, grad_out):
    shape = queries.shape
    tokens, local_heads, depth = shape[2:]
    heads = local_heads // 2
    columns = tokens // QUARTERS
    chunks = heads * QUARTERS
    flat = [
        pltpu.with_memory_space_constraint(x.reshape(tokens, local_heads, depth), pltpu.HBM)
        for x in (queries, key_vecs, value_vecs, grad_out)
    ]
    hbm = pl.BlockSpec(memory_space=pltpu.HBM)
    vmem = pl.BlockSpec(memory_space=pltpu.VMEM)
    two = pltpu.VMEM((chunks, 2, columns, depth), BF16)
    few = pltpu.VMEM((heads, 2, columns, depth), BF16)
    four = pltpu.VMEM((chunks, 4, columns, depth), BF16)
    row_buf = pltpu.VMEM((heads, 4, tokens, depth), BF16)
    flat_rows = pltpu.VMEM((chunks, 8, columns), F32)
    dma = pltpu.SemaphoreType.DMA
    joined = pl.pallas_call(
        kernel,
        out_shape=[pltpu.VMEM((tokens, local_heads, depth), BF16)] * 4,
        in_specs=[hbm] * 4,
        out_specs=[vmem] * 4,
        scratch_shapes=[
            pltpu.VMEM((4, tokens, local_heads, depth), BF16),
            pltpu.VMEM((4, columns * local_heads, depth), F32),
            row_buf, four, row_buf, four,
            pltpu.VMEM((2, tokens // 2, depth), F32),
            pltpu.VMEM((chunks, 2, columns, depth), F32),
            two, two, few, two, flat_rows, two, two, two, few, flat_rows,
            pltpu.VMEM((2, chunks, 8, columns), F32), flat_rows,
            two, two, two,
            dma((4, QUARTERS)), dma((7, chunks)), dma((10, chunks)),
        ],
        compiler_params=pltpu.CompilerParams(
            collective_id=0, has_side_effects=True, vmem_limit_bytes=44 * 1024 * 1024
        ),
    )(*flat)
    results = pl.pallas_call(
        store_kernel,
        out_shape=[jax.ShapeDtypeStruct((tokens, local_heads, depth), BF16)] * 4,
        in_specs=[vmem] * 4,
        out_specs=[pl.BlockSpec(memory_space=pl.ANY)] * 4,
        scratch_shapes=[dma((4,))],
        compiler_params=pltpu.CompilerParams(vmem_limit_bytes=2 * 1024 * 1024),
    )(*joined)
    return tuple(x.reshape(shape) for x in results)


def causal(length):
    positions = jnp.arange(length)
    return positions[None, :] <= positions[:, None]


def attend(query_in, key_in, value_in, grad_in, layout, allowed):
    scaling = 1.0 / math.sqrt(query_in.shape[-1])
    key_form = layout.replace("q", "k")
    scores = (
        jnp.einsum(
            layout + "," + key_form + "->bxhqk",
            query_in,
            key_in,
            preferred_element_type=jnp.float32,
        )
        * scaling
    )
    scores = jnp.where(allowed, scores, -1e30)
    highest = jnp.max(scores, axis=-1, keepdims=True)
    weight_sum = jnp.sum(jnp.exp(scores - highest), axis=-1, keepdims=True)
    log_total = highest + jnp.log(weight_sum)
    weights = jnp.where(allowed, jnp.exp(scores - log_total), 0.0)
    rounded = weights.astype(jnp.bfloat16)
    output = jnp.einsum(
        "bxhqk," + key_form + "->" + layout, rounded, value_in, preferred_element_type=jnp.float32
    ).astype(jnp.bfloat16)
    row_dots = jnp.einsum(
        layout + "," + layout + "->bxhq", grad_in, output, preferred_element_type=jnp.float32
    )
    dprobs = jnp.einsum(
        layout + "," + key_form + "->bxhqk", grad_in, value_in, preferred_element_type=jnp.float32
    )
    dscores = (weights * (dprobs - row_dots[..., None]) * scaling).astype(jnp.bfloat16)
    grad_query = jnp.einsum(
        "bxhqk," + key_form + "->" + layout, dscores, key_in, preferred_element_type=jnp.float32
    ).astype(jnp.bfloat16)
    grad_key = jnp.einsum(
        "bxhqk," + layout + "->" + key_form, dscores, query_in, preferred_element_type=jnp.float32
    )
    grad_value = jnp.einsum(
        "bxhqk," + layout + "->" + key_form, rounded, grad_in, preferred_element_type=jnp.float32
    )
    return (output, grad_query, grad_key, grad_value)


def merge_heads(first_part, second_part):
    stacked = jnp.stack((first_part, second_part), axis=4)
    shape = first_part.shape
    return stacked.reshape(shape[:3] + (2 * shape[3], shape[4]))


def per_device(queries, key_vecs, value_vecs, grad_out):
    arrays = (queries, key_vecs, value_vecs, grad_out)
    row_parts = tuple((array[:, :, :, 0::2] for array in arrays))
    col_parts = tuple((array[:, :, :, 1::2] for array in arrays))
    row_local = attend(
        row_parts[0], row_parts[1], row_parts[2], row_parts[3], "bxqhd", causal(queries.shape[2])
    )
    row_results = (
        row_local[0],
        row_local[1],
        row_local[2].astype(jnp.bfloat16),
        row_local[3].astype(jnp.bfloat16),
    )
    local_rows = col_parts[0].shape[1]
    gathered = (
        lax.all_gather(col_parts[1], "ctx", axis=1, tiled=True),
        lax.all_gather(col_parts[2], "ctx", axis=1, tiled=True),
    )
    query_rows = lax.axis_index("ctx") * local_rows + jnp.arange(local_rows)
    key_rows = jnp.arange(gathered[0].shape[1])
    allowed = key_rows[None, :] <= query_rows[:, None]
    col_local = attend(col_parts[0], gathered[0], gathered[1], col_parts[3], "bqxhd", allowed)
    summed = (
        lax.psum_scatter(col_local[2], "ctx", scatter_dimension=1, tiled=True),
        lax.psum_scatter(col_local[3], "ctx", scatter_dimension=1, tiled=True),
    )
    col_results = (
        col_local[0],
        col_local[1],
        summed[0].astype(jnp.bfloat16),
        summed[1].astype(jnp.bfloat16),
    )
    return (
        merge_heads(row_results[0], col_results[0]),
        merge_heads(row_results[1], col_results[1]),
        merge_heads(row_results[2], col_results[2]),
        merge_heads(row_results[3], col_results[3]),
    )


def solution(mesh):
    body = fused if mesh.shape["ctx"] == 4 else per_device
    placed = (
        P(("groups", "dp"), "ctx", None, "head", None),
        P(("groups", "dp"), "ctx", None, "head", None),
        P(("groups", "dp"), "ctx", None, "head", None),
        P(("groups", "dp"), "ctx", None, "head", None),
    )
    return jax.shard_map(
        body,
        mesh=mesh,
        in_specs=placed,
        out_specs=(
            P(("groups", "dp"), "ctx", None, "head", None),
            P(("groups", "dp"), "ctx", None, "head", None),
            P(("groups", "dp"), "ctx", None, "head", None),
            P(("groups", "dp"), "ctx", None, "head", None),
        ),
        check_vma=False,
    )
```

```python
import functools
import math

import jax
import jax.numpy as jnp
from jax import lax
from jax.experimental import pallas as pl
from jax.experimental.pallas import tpu as pltpu
from jax.sharding import PartitionSpec as P

MESH = pl.DeviceIdType.MESH
F32 = jnp.float32
BF16 = jnp.bfloat16
NT = (((1,), (1,)), ((), ()))
NN = (((1,), (0,)), ((), ()))
TN = (((0,), (0,)), ((), ()))


def mm(a, b, dims):
    return lax.dot_general(a, b, dims, preferred_element_type=F32)


def row_piece(buf, acc, stage, i, b, tokens, depth):
    scaling = 1.0 / math.sqrt(depth)
    block = tokens // 2
    rows = pl.ds(b * block, block)
    span = (b + 1) * block
    q = buf[i, Q, rows]
    g = buf[i, G, rows]
    k = buf[i, K, pl.ds(0, span)]
    v = buf[i, V, pl.ds(0, span)]
    s = mm(q, k, NT) * scaling
    qpos = lax.broadcasted_iota(jnp.int32, (block, span), 0) + b * block
    kpos = lax.broadcasted_iota(jnp.int32, (block, span), 1)
    s = jnp.where(kpos <= qpos, s, -1e30)
    top = jnp.max(s, axis=-1, keepdims=True)
    e = jnp.exp(s - top)
    p = e * (1.0 / jnp.sum(e, axis=-1, keepdims=True))
    pb = p.astype(BF16)
    o = mm(pb, v, NN).astype(BF16)
    dots = jnp.sum(g.astype(F32) * o.astype(F32), axis=-1, keepdims=True)
    dp = mm(g, v, NT)
    ds = (p * (dp - dots) * scaling).astype(BF16)
    stage[i, 0, rows] = o
    stage[i, 1, rows] = mm(ds, k, NN).astype(BF16)
    dk = mm(ds, q, TN)
    dv = mm(pb, g, TN)
    if b == 1:
        acc[0] = dk[:block]
        acc[1] = dv[:block]
        stage[i, 2, rows] = dk[block:].astype(BF16)
        stage[i, 3, rows] = dv[block:].astype(BF16)
    else:
        stage[i, 2, rows] = (acc[0] + dk).astype(BF16)
        stage[i, 3, rows] = (acc[1] + dv).astype(BF16)


def dot(a, b):
    return jnp.sum(a * b, axis=-1, keepdims=True)


def add_up(terms):
    return functools.reduce(jnp.add, terms)


def attend_to(q, g, keys, scaling, rest=None):
    s = [dot(q, k) * scaling for k, _ in keys]
    dp = [dot(g, v) for _, v in keys]
    if rest is not None:
        s, dp = s + [rest[0]], dp + [rest[1]]
    top = functools.reduce(jnp.maximum, s)
    e = [jnp.exp(x - top) for x in s]
    total = add_up(e)
    inverse = 1.0 / total
    p = [x * inverse for x in e]
    dots = add_up([x * y for x, y in zip(p, dp)])
    ds = [x * (y - dots) * scaling for x, y in zip(p, dp)]
    o = add_up([x * kv[1] for x, kv in zip(p, keys)])
    dq = add_up([x * kv[0] for x, kv in zip(ds, keys)])
    return o, dq, p, ds, top + jnp.log(total), dots


def to_rows(columns):
    tokens = columns[0].shape[0]
    lane = lax.broadcasted_iota(jnp.int32, (tokens, 128), 1)
    wide = jnp.broadcast_to(columns[0], (tokens, 128))
    for i, x in enumerate(columns[1:], 1):
        wide = jnp.where(lane == i, x, wide)
    return jnp.transpose(wide)[:8]


def stack_rows(rows):
    index = lax.broadcasted_iota(jnp.int32, (8, rows[0].shape[1]), 0)
    out = jnp.broadcast_to(rows[0], index.shape)
    for i, x in enumerate(rows[1:], 1):
        out = jnp.where(index == i, x, out)
    return out


def to_columns(rows, count):
    turned = jnp.transpose(jnp.concatenate([rows] * 16, axis=0))
    return [turned[:, i : i + 1] for i in range(count)]


Q, G, K, V = 0, 1, 2, 3
QUARTERS = 4
KV0, KV1, QG2, QG3, SC, GA, GB, OD_A, OD_B, SCD = range(10)


def each(first, last, body):
    def step(i, _):
        body(i)
        return 0

    lax.fori_loop(first, last, step, 0)


def kernel(
    q_ref, k_ref, v_ref, g_ref, o_out, dq_out, dk_out, dv_out, late,
    fetched, wide, rows_in, cols_in, rows_stage, joined, acc, own_grads,
    kv0, kv1, qg2, qg3, sc, grads_a, grads_b, od_a, od_b, scd,
    sc_stage, scd_stage, send_a, send_b, send_c,
    load, sent, got,
):
    tokens, local_heads, depth = q_ref.shape
    heads = local_heads // 2
    columns = tokens // QUARTERS
    chunks = heads * QUARTERS
    scaling = 1.0 / math.sqrt(depth)
    me = lax.axis_index("ctx")
    refs = (q_ref, g_ref, k_ref, v_ref)
    outs = (o_out, dq_out, dk_out, dv_out)
    shift = jnp.where(me < 2, 1, 0)
    late_quarter = jnp.where(me < 2, QUARTERS - 1, 0)
    late_first = jnp.where(me < 2, 2, 0)

    barrier = pltpu.get_barrier_semaphore()

    def greet(target):
        pl.semaphore_signal(barrier, inc=1, device_id={"ctx": target}, device_id_type=MESH)

    @pl.when(me == 1)
    def _():
        greet(0)
        greet(2)

    @pl.when(me == 2)
    def _():
        greet(1)
        greet(3)

    def turn(step):
        return lax.rem(step + shift, QUARTERS)

    def fetch(at, quarter):
        part = pl.ds(quarter * columns, columns)
        return pltpu.make_async_copy(refs[at].at[part], fetched.at[at, part], load.at[at, quarter])

    def fetch_first(arrays):
        for at in arrays:
            fetch(at, turn(0)).start()

    def fetch_rest(arrays, others):
        for at in others:
            fetch(at, turn(0)).start()

        def later(step):
            for at in arrays + others:
                fetch(at, turn(step)).start()

        each(1, QUARTERS, later)

    @pl.when(me < 2)
    def _():
        fetch_first((K, V))

    @pl.when(me >= 2)
    def _():
        fetch_first((Q, G))

    def remote(src, dst, send, recv, c, target):
        return pltpu.make_async_remote_copy(
            src_ref=src, dst_ref=dst, send_sem=sent.at[send, c], recv_sem=got.at[recv, c],
            device_id={"ctx": target}, device_id_type=MESH,
        )

    def pair_of(c, first):
        return cols_in.at[c, pl.ds(first, 2)]

    def split(at, quarter):
        fetch(at, quarter).wait()
        x = fetched[at, pl.ds(quarter * columns, columns)].astype(F32)
        wide[at] = x.reshape(columns * local_heads, depth)
        for h in range(local_heads):
            x = wide[at, pl.ds(h, columns, stride=local_heads)].astype(BF16)
            if h % 2 == 0:
                rows_in[h // 2, at, pl.ds(quarter * columns, columns)] = x
            else:
                cols_in[quarter * heads + h // 2, at] = x

    def place_rows(quarter):
        part = pl.ds(quarter * columns, columns)
        for a in range(4):
            for h in range(heads):
                x = rows_stage[h, a, part].astype(F32)
                joined[a, quarter, pl.ds(2 * h, columns, stride=local_heads)] = x

        @pl.when(quarter == late_quarter)
        def _():
            for a in range(2):
                for h in range(heads):
                    x = rows_stage[h, late_first + a, part].astype(F32)
                    late[a, pl.ds(2 * h, columns, stride=local_heads)] = x

    def emit_late(c, values):
        for a, x in enumerate(values):
            late[a, pl.ds(2 * (c % heads) + 1, columns, stride=local_heads)] = x

    def emit(c, first, values):
        for a, x in enumerate(values, first):
            spots = pl.ds(2 * (c % heads) + 1, columns, stride=local_heads)
            joined[a, c // heads, spots] = x.astype(F32)

    def join(a, quarter):
        part = pl.ds(quarter * columns, columns)
        outs[a][part] = joined[a, quarter].reshape(columns, local_heads, depth).astype(BF16)

    def vectors(buf, c):
        return [buf[c, a].astype(F32) for a in range(buf.shape[1])]

    def put(ref, c, first, values):
        for a, x in enumerate(values):
            ref[c, first + a] = x.astype(ref.dtype)

    def kv0_copy(c):
        return remote(pair_of(c, K), kv0.at[c], 0, KV0, c, 1)

    def kv0_forward(c):
        return remote(kv0.at[c], kv0.at[c], 0, KV0, c, 2)

    def kv1_copy(c):
        return remote(pair_of(c, K), kv1.at[c], 1, KV1, c, 2)

    def grads_1_to_0(c):
        return remote(send_a.at[c], grads_b.at[c], 2, GB, c, 0)

    def od_1_to_2(c):
        return remote(send_b.at[c], od_b.at[c], 3, OD_B, c, 2)

    def od_1_to_3(c):
        return remote(send_c.at[c], od_b.at[c], 4, OD_B, c, 3)

    def scd_1_to_2(c):
        return remote(scd_stage.at[c], scd.at[c], 5, SCD, c, 2)

    def scd_forward(c):
        return remote(scd.at[c], scd.at[c], 6, SCD, c, 3)

    def qg2_copy(c):
        return remote(pair_of(c, Q), qg2.at[c], 0, QG2, c, 1)

    def qg3_forward(c):
        return remote(qg3.at[c], qg3.at[c], 1, QG3, c, 1)

    def sc_2_to_1(c):
        return remote(sc_stage.at[1, c], sc.at[c], 2, SC, c, 1)

    def grads_2_to_0(c):
        return remote(send_a.at[c], grads_a.at[c], 3, GA, c, 0)

    def grads_2_to_1(c):
        return remote(send_b.at[c], grads_a.at[c], 4, GA, c, 1)

    def od_2_to_3(c):
        return remote(send_c.at[c], od_a.at[c], 5, OD_A, c, 3)

    def scd_2_to_3(c):
        return remote(scd_stage.at[c], scd.at[c], 6, SCD, c, 3)

    def qg3_copy(c):
        return remote(pair_of(c, Q), qg3.at[c], 0, QG3, c, 2)

    def sc_3_to_2(c):
        return remote(sc_stage.at[0, c], sc.at[c], 1, SC, c, 2)

    @pl.when(me == 0)
    def _():
        def go(step):
            quarter = turn(step)
            split(K, quarter)
            split(V, quarter)

            @pl.when(step == 0)
            def _():
                pl.semaphore_wait(barrier, 1)

            each(0, heads, lambda i: kv0_copy(quarter * heads + i).start())

            @pl.when(step == 0)
            def _():
                fetch_rest((K, V), (Q, G))

            split(Q, quarter)
            split(G, quarter)

        each(0, QUARTERS, go)

    @pl.when(me == 1)
    def _():
        split(K, 1)
        split(V, 1)
        pl.semaphore_wait(barrier, 1)
        kv1_copy(heads).start()
        kv1_copy(heads + 1).start()
        fetch_rest((K, V), (Q, G))

    @pl.when(me == 2)
    def _():
        split(Q, 0)
        split(G, 0)
        pl.semaphore_wait(barrier, 1)
        each(0, heads, lambda c: qg2_copy(c).start())
        fetch_rest((Q, G), (K, V))
        split(K, 0)
        split(V, 0)

        def pass_on(c):
            qg3_copy(c).wait_recv()
            qg3_forward(c).start()
            q, g, k, v = vectors(cols_in, c)
            q3, g3 = vectors(qg3, c)
            own = to_rows([dot(q, k) * scaling, dot(g, v), dot(q3, k) * scaling, dot(g3, v)])
            sc_stage[0, c] = own

            @pl.when(c < QUARTERS - 1)
            def _():
                for at in range(4):
                    split(at, c + 1)

        each(0, heads, pass_on)

        def merge(c):
            sc_3_to_2(c).wait_recv()
            own, far = sc_stage[0, c], sc[c]
            s32, dp32, s33, dp33 = own[2:3], own[3:4], far[0:1], far[1:2]
            top = jnp.maximum(s32, s33)
            e32, e33 = jnp.exp(s32 - top), jnp.exp(s33 - top)
            total = e32 + e33
            mean = (e32 * dp32 + e33 * dp33) / total
            sc_stage[1, c] = stack_rows([own[0:1], own[1:2], top + jnp.log(total), mean])
            sc_2_to_1(c).start()

        each(0, heads, merge)

    @pl.when(me == 3)
    def _():
        def go(quarter):
            split(Q, quarter)
            split(G, quarter)

            @pl.when(quarter == 0)
            def _():
                pl.semaphore_wait(barrier, 1)
                each(0, heads, lambda c: qg3_copy(c).start())
                fetch_rest((Q, G), (K, V))

            split(K, quarter)
            split(V, quarter)

            def scores(i):
                c = quarter * heads + i

                @pl.when(quarter > 0)
                def _():
                    qg3_copy(c).start()

                q, g, k, v = vectors(cols_in, c)
                sc_stage[0, c] = to_rows([dot(q, k) * scaling, dot(g, v)])
                sc_3_to_2(c).start()

            each(0, heads, scores)

        each(0, QUARTERS, go)

    def chunk_0(t):
        c = jnp.where(t < 2 * heads, t + heads, jnp.where(t < 3 * heads, t - 2 * heads, t))
        q, g, k, v = vectors(cols_in, c)
        o, dq, p, ds, _, _ = attend_to(q, g, [(k, v)], scaling)
        emit(c, 0, (o, dq))
        kv0_copy(c).wait_send()

        @pl.when(t == chunks - 1)
        def _():
            join(0, 3)
            join(1, 3)

        grads_1_to_0(c).wait_recv()
        near = vectors(grads_b, c)
        total = (ds[0] * q + near[0], p[0] * g + near[1])

        @pl.when(c < heads)
        def _():
            emit(c, 2, total)

        @pl.when(c >= heads)
        def _():
            grads_2_to_0(c).wait_recv()
            far = vectors(grads_a, c)
            whole = (total[0] + far[0], total[1] + far[1])

            @pl.when(c < chunks - heads)
            def _():
                emit(c, 2, whole)

            @pl.when(c >= chunks - heads)
            def _():
                emit_late(c, whole)

    def chunk_1a(t):
        c = t + heads
        kv0_copy(c).wait_recv()
        kv0_forward(c).start()

        @pl.when((t % 2 == 1) & (t <= 5))
        def _():
            split(K, (t // 2 + 2) % QUARTERS)
            split(V, (t // 2 + 2) % QUARTERS)

        @pl.when(c + 2 < chunks)
        def _():
            kv1_copy(c + 2).start()

        @pl.when((t % 2 == 0) & (t <= 6))
        def _():
            split(Q, (t // 2 + 1) % QUARTERS)
            split(G, (t // 2 + 1) % QUARTERS)

        q, g, k, v = vectors(cols_in, c)
        k0, v0 = vectors(kv0, c)
        o, dq, p, ds, _, _ = attend_to(q, g, [(k0, v0), (k, v)], scaling)
        put(send_a, c, 0, (ds[0] * q, p[0] * g))
        grads_1_to_0(c).start()
        emit(c, 0, (o, dq))
        put(own_grads, c, 0, (ds[1] * q, p[1] * g))

    def chunk_1b(c):
        kv0_copy(c).wait_recv()
        qg2_copy(c).wait_recv()
        qg3_copy(c).wait_recv()
        sc_2_to_1(c).wait_recv()
        q, g, k, v = vectors(cols_in, c)
        k0, v0 = vectors(kv0, c)
        keys = [(k0, v0), (k, v)]
        rest = to_columns(sc[c], 4)
        q2, g2 = vectors(qg2, c)
        o2, dq2, p2, ds2, lse2, dots2 = attend_to(q2, g2, keys, scaling, rest[:2])
        q3, g3 = vectors(qg3, c)
        o3, dq3, p3, ds3, lse3, dots3 = attend_to(q3, g3, keys, scaling, rest[2:])
        scd_stage[c] = to_rows([lse3, dots3, lse2, dots2])
        scd_1_to_2(c).start()
        put(send_b, c, 0, (o2, dq2))
        put(send_c, c, 0, (o3, dq3))

        o, dq, p, ds, _, _ = attend_to(q, g, keys, scaling)
        emit(c, 0, (o, dq))
        dk = [ds[j] * q + ds2[j] * q2 + ds3[j] * q3 for j in range(2)]
        dv = [p[j] * g + p2[j] * g2 + p3[j] * g3 for j in range(2)]
        put(send_a, c, 0, (dk[0], dv[0]))
        grads_1_to_0(c).start()
        emit(c, 2, (dk[1], dv[1]))

    def chunk_2a(t):
        c = t + heads
        kv1_copy(c).wait_recv()
        kv0_forward(c).wait_recv()
        qg3_copy(c).wait_recv()
        sc_3_to_2(c).wait_recv()
        q, g, k, v = vectors(cols_in, c)
        q3, g3 = vectors(qg3, c)
        k0, v0 = vectors(kv0, c)
        k1, v1 = vectors(kv1, c)
        keys = [(k0, v0), (k1, v1), (k, v)]
        rest = to_columns(sc[c], 2)
        o, dq, p, ds, _, _ = attend_to(q, g, keys, scaling)
        o3, dq3, p3, ds3, lse3, dots3 = attend_to(q3, g3, keys, scaling, rest)
        dk = [ds[j] * q + ds3[j] * q3 for j in range(3)]
        dv = [p[j] * g + p3[j] * g3 for j in range(3)]
        put(send_a, c, 0, (dk[0], dv[0]))
        grads_2_to_0(c).start()
        put(send_b, c, 0, (dk[1], dv[1]))

        @pl.when(t >= LAG)
        def _():
            grads_2_to_1(c - LAG).start()

        @pl.when(t == 3 * heads - 1)
        def _():
            for late in range(LAG):
                grads_2_to_1(chunks - LAG + late).start()

        scd_stage[c] = to_rows([lse3, dots3])
        scd_2_to_3(c).start()
        put(send_c, c, 0, (o3, dq3))
        od_2_to_3(c).start()
        emit(c, 0, (o, dq, dk[2], dv[2]))

    def chunk_2b(c):
        scd_1_to_2(c).wait_recv()
        scd_forward(c).start()
        own, far = sc_stage[0, c], scd[c]
        p3 = jnp.exp(own[2:3] - far[0:1])
        ds3 = p3 * (own[3:4] - far[1:2]) * scaling
        p2 = jnp.exp(own[0:1] - far[2:3])
        ds2 = p2 * (own[1:2] - far[3:4]) * scaling
        p3, ds3, p2, ds2 = to_columns(stack_rows([p3, ds3, p2, ds2]), 4)
        q, g, k, v = vectors(cols_in, c)
        put(send_c, c, 0, (p3 * v, ds3 * k))
        od_2_to_3(c).start()
        q3, g3 = vectors(qg3, c)
        emit(c, 2, (ds2 * q + ds3 * q3, p2 * g + p3 * g3))
        put(own_grads, c, 0, (p2 * v, ds2 * k))

    def finish_2(c):
        qg2_copy(c).wait_send()
        qg3_forward(c).wait_send()
        sc_2_to_1(c).wait_send()

        def done(late):
            grads_2_to_0(late).wait_send()
            grads_2_to_1(late).wait_send()
            scd_2_to_3(late).wait_send()
            od_2_to_3(late).wait_send()

        each(heads + 3 * c, heads + 3 * c + 3, done)
        scd_forward(c).wait_send()
        od_2_to_3(c).wait_send()

        @pl.when(c > 0)
        def _():
            for a in range(4):
                join(a, c)

        @pl.when(c == 0)
        def _():
            join(2, 0)
            join(3, 0)

        od_1_to_2(c).wait_recv()
        far = vectors(od_b, c)
        emit_late(c, [own_grads[c, a] + far[a] for a in range(2)])

    def chunk_3(c):
        scd_2_to_3(c).wait_recv()
        own, far = sc_stage[0, c], scd[c]
        p = jnp.exp(own[0:1] - far[0:1])
        ds = p * (own[1:2] - far[1:2]) * scaling
        p, ds = to_columns(stack_rows([p, ds]), 2)
        q, g, k, v = vectors(cols_in, c)
        emit(c, 2, (ds * q, p * g))
        qg3_copy(c).wait_send()
        sc_3_to_2(c).wait_send()

        @pl.when(c == heads - 1)
        def _():
            join(2, 0)
            join(3, 0)

        od_2_to_3(c).wait_recv()
        near = vectors(od_a, c)
        total = (p * v + near[0], ds * k + near[1])

        @pl.when(c >= heads)
        def _():
            emit(c, 0, total)

        @pl.when(c < heads)
        def _():
            od_1_to_3(c).wait_recv()
            far = vectors(od_b, c)
            emit_late(c, (total[0] + far[0], total[1] + far[1]))

    ends = (me == 0) | (me == 3)
    first_row = jnp.where(me == 1, 3 * heads, jnp.where(me == 2, 1, -3 * heads))
    first_step = jnp.where(ends, -3 * heads, 0)
    steps = jnp.where(me == 1, chunks + 2 * heads, chunks)

    def body(t):
        piece = t - first_row
        here = (piece >= 0) & (piece < 2 * heads)

        @pl.when(here & (piece % 2 == 0))
        def _():
            row_piece(rows_in, acc, rows_stage, piece // 2, 1, tokens, depth)

        @pl.when(here & (piece % 2 == 1))
        def _():
            row_piece(rows_in, acc, rows_stage, piece // 2, 0, tokens, depth)

        rest = piece - 2 * heads

        @pl.when((rest >= 0) & (rest < QUARTERS))
        def _():
            place_rows(rest)

        @pl.when(ends & ((t == heads) | (t == 2 * heads) | (t == 3 * heads)))
        def _():
            quarter = jnp.where((me == 0) & (t == 3 * heads), 0, t // heads)
            for a in range(4):
                join(a, quarter)

        @pl.when((me == 0) & (t >= 0))
        def _():
            chunk_0(t)

        @pl.when((me == 1) & (t >= 0) & (t < 3 * heads))
        def _():
            chunk_1a(t)

        @pl.when((me == 1) & (t >= FIRST_B) & (t < FIRST_B + heads))
        def _():
            chunk_1b(t - FIRST_B)

        @pl.when((me == 1) & (t == 3 * heads - 1))
        def _():
            each(0, heads, lambda c: od_1_to_3(c).start())
            each(0, heads, lambda c: od_1_to_2(c).start())

        @pl.when((me == 2) & (t < 3 * heads))
        def _():
            chunk_2a(t)

        @pl.when((me == 2) & (t >= 2 * heads) & (t < 3 * heads))
        def _():
            chunk_2b(t - 2 * heads)

        @pl.when((me == 3) & (t >= 0))
        def _():
            chunk_3((t + heads) % chunks)

    each(first_step, steps, body)

    @pl.when(me == 1)
    def _():
        join(2, 0)
        join(3, 0)

        def join_early(quarter):
            join(0, quarter)
            join(1, quarter)

        each(0, QUARTERS, join_early)

        def finish(c):
            kv0_forward(c).wait_send()
            kv1_copy(c).wait_send()
            grads_1_to_0(c).wait_send()

            @pl.when(c == chunks - 1)
            def _():
                each(0, heads, done_b)

            grads_2_to_1(c).wait_recv()
            far = vectors(grads_a, c)
            total = [own_grads[c, a] + far[a] for a in range(2)]

            @pl.when(c < chunks - heads)
            def _():
                emit(c, 2, total)

            @pl.when(c >= chunks - heads)
            def _():
                emit_late(c, total)

            @pl.when((c % heads == heads - 1) & (c < chunks - 1))
            def _():
                join(2, c // heads)
                join(3, c // heads)

        def done_b(c):
            grads_1_to_0(c).wait_send()
            od_1_to_2(c).wait_send()
            od_1_to_3(c).wait_send()
            scd_1_to_2(c).wait_send()

        each(heads, chunks, finish)

    @pl.when(me == 2)
    def _():
        each(0, heads, finish_2)


LAG = 3
FIRST_B = 7


def store_kernel(*refs):
    ins, late, outs, last, leave = refs[:4], refs[4], refs[5:9], refs[9], refs[10]
    tokens, local_heads, depth = ins[0].shape
    columns = tokens // QUARTERS
    me = lax.axis_index("ctx")

    def send(a, first, count):
        part = pl.ds(first * columns, count * columns)
        return pltpu.make_async_copy(ins[a].at[part], outs[a].at[part], leave.at[a])

    def send_last(a, quarter):
        part = pl.ds(quarter * columns, columns)
        return pltpu.make_async_copy(last.at[a % 2], outs[a].at[part], leave.at[4 + a % 2])

    def store(arrays, others, first, quarter):
        whole = [send(a, 0, QUARTERS) for a in others] + [send(a, first, QUARTERS - 1) for a in arrays]
        for copy in whole:
            copy.start()
        for i, a in enumerate(arrays):
            last[i] = late[i].reshape(columns, local_heads, depth).astype(BF16)
            send_last(a, quarter).start()
        for copy in whole:
            copy.wait()
        for a in arrays:
            send_last(a, quarter).wait()

    @pl.when(me < 2)
    def _():
        store((2, 3), (0, 1), 0, QUARTERS - 1)

    @pl.when(me >= 2)
    def _():
        store((0, 1), (2, 3), 1, 0)


def fused(queries, key_vecs, value_vecs, grad_out):
    shape = queries.shape
    tokens, local_heads, depth = shape[2:]
    heads = local_heads // 2
    columns = tokens // QUARTERS
    chunks = heads * QUARTERS
    flat = [
        pltpu.with_memory_space_constraint(x.reshape(tokens, local_heads, depth), pltpu.HBM)
        for x in (queries, key_vecs, value_vecs, grad_out)
    ]
    hbm = pl.BlockSpec(memory_space=pltpu.HBM)
    vmem = pl.BlockSpec(memory_space=pltpu.VMEM)
    two = pltpu.VMEM((chunks, 2, columns, depth), BF16)
    few = pltpu.VMEM((heads, 2, columns, depth), BF16)
    four = pltpu.VMEM((chunks, 4, columns, depth), BF16)
    row_buf = pltpu.VMEM((heads, 4, tokens, depth), BF16)
    flat_rows = pltpu.VMEM((chunks, 8, columns), F32)
    dma = pltpu.SemaphoreType.DMA
    parts = pl.pallas_call(
        kernel,
        out_shape=[pltpu.VMEM((tokens, local_heads, depth), BF16)] * 4
        + [pltpu.VMEM((2, columns * local_heads, depth), F32)],
        in_specs=[hbm] * 4,
        out_specs=[vmem] * 5,
        scratch_shapes=[
            pltpu.VMEM((4, tokens, local_heads, depth), BF16),
            pltpu.VMEM((4, columns * local_heads, depth), F32),
            row_buf, four, row_buf,
            pltpu.VMEM((4, QUARTERS, columns * local_heads, depth), F32),
            pltpu.VMEM((2, tokens // 2, depth), F32),
            pltpu.VMEM((chunks, 2, columns, depth), F32),
            two, two, few, two, flat_rows, two, two, two, few, flat_rows,
            pltpu.VMEM((2, chunks, 8, columns), F32), flat_rows,
            two, two, two,
            dma((4, QUARTERS)), dma((7, chunks)), dma((10, chunks)),
        ],
        compiler_params=pltpu.CompilerParams(
            collective_id=0, has_side_effects=True, vmem_limit_bytes=44 * 1024 * 1024
        ),
    )(*flat)
    results = pl.pallas_call(
        store_kernel,
        out_shape=[jax.ShapeDtypeStruct((tokens, local_heads, depth), BF16)] * 4,
        in_specs=[vmem] * 5,
        out_specs=[pl.BlockSpec(memory_space=pl.ANY)] * 4,
        scratch_shapes=[pltpu.VMEM((2, columns, local_heads, depth), BF16), dma((6,))],
        compiler_params=pltpu.CompilerParams(vmem_limit_bytes=2 * 1024 * 1024),
    )(*parts)
    return tuple(x.reshape(shape) for x in results)


def causal(length):
    positions = jnp.arange(length)
    return positions[None, :] <= positions[:, None]


def attend(query_in, key_in, value_in, grad_in, layout, allowed):
    scaling = 1.0 / math.sqrt(query_in.shape[-1])
    key_form = layout.replace("q", "k")
    scores = (
        jnp.einsum(
            layout + "," + key_form + "->bxhqk",
            query_in,
            key_in,
            preferred_element_type=jnp.float32,
        )
        * scaling
    )
    scores = jnp.where(allowed, scores, -1e30)
    highest = jnp.max(scores, axis=-1, keepdims=True)
    weight_sum = jnp.sum(jnp.exp(scores - highest), axis=-1, keepdims=True)
    log_total = highest + jnp.log(weight_sum)
    weights = jnp.where(allowed, jnp.exp(scores - log_total), 0.0)
    rounded = weights.astype(jnp.bfloat16)
    output = jnp.einsum(
        "bxhqk," + key_form + "->" + layout, rounded, value_in, preferred_element_type=jnp.float32
    ).astype(jnp.bfloat16)
    row_dots = jnp.einsum(
        layout + "," + layout + "->bxhq", grad_in, output, preferred_element_type=jnp.float32
    )
    dprobs = jnp.einsum(
        layout + "," + key_form + "->bxhqk", grad_in, value_in, preferred_element_type=jnp.float32
    )
    dscores = (weights * (dprobs - row_dots[..., None]) * scaling).astype(jnp.bfloat16)
    grad_query = jnp.einsum(
        "bxhqk," + key_form + "->" + layout, dscores, key_in, preferred_element_type=jnp.float32
    ).astype(jnp.bfloat16)
    grad_key = jnp.einsum(
        "bxhqk," + layout + "->" + key_form, dscores, query_in, preferred_element_type=jnp.float32
    )
    grad_value = jnp.einsum(
        "bxhqk," + layout + "->" + key_form, rounded, grad_in, preferred_element_type=jnp.float32
    )
    return (output, grad_query, grad_key, grad_value)


def merge_heads(first_part, second_part):
    stacked = jnp.stack((first_part, second_part), axis=4)
    shape = first_part.shape
    return stacked.reshape(shape[:3] + (2 * shape[3], shape[4]))


def per_device(queries, key_vecs, value_vecs, grad_out):
    arrays = (queries, key_vecs, value_vecs, grad_out)
    row_parts = tuple((array[:, :, :, 0::2] for array in arrays))
    col_parts = tuple((array[:, :, :, 1::2] for array in arrays))
    row_local = attend(
        row_parts[0], row_parts[1], row_parts[2], row_parts[3], "bxqhd", causal(queries.shape[2])
    )
    row_results = (
        row_local[0],
        row_local[1],
        row_local[2].astype(jnp.bfloat16),
        row_local[3].astype(jnp.bfloat16),
    )
    local_rows = col_parts[0].shape[1]
    gathered = (
        lax.all_gather(col_parts[1], "ctx", axis=1, tiled=True),
        lax.all_gather(col_parts[2], "ctx", axis=1, tiled=True),
    )
    query_rows = lax.axis_index("ctx") * local_rows + jnp.arange(local_rows)
    key_rows = jnp.arange(gathered[0].shape[1])
    allowed = key_rows[None, :] <= query_rows[:, None]
    col_local = attend(col_parts[0], gathered[0], gathered[1], col_parts[3], "bqxhd", allowed)
    summed = (
        lax.psum_scatter(col_local[2], "ctx", scatter_dimension=1, tiled=True),
        lax.psum_scatter(col_local[3], "ctx", scatter_dimension=1, tiled=True),
    )
    col_results = (
        col_local[0],
        col_local[1],
        summed[0].astype(jnp.bfloat16),
        summed[1].astype(jnp.bfloat16),
    )
    return (
        merge_heads(row_results[0], col_results[0]),
        merge_heads(row_results[1], col_results[1]),
        merge_heads(row_results[2], col_results[2]),
        merge_heads(row_results[3], col_results[3]),
    )


def solution(mesh):
    body = fused if mesh.shape["ctx"] == 4 else per_device
    placed = (
        P(("groups", "dp"), "ctx", None, "head", None),
        P(("groups", "dp"), "ctx", None, "head", None),
        P(("groups", "dp"), "ctx", None, "head", None),
        P(("groups", "dp"), "ctx", None, "head", None),
    )
    return jax.shard_map(
        body,
        mesh=mesh,
        in_specs=placed,
        out_specs=(
            P(("groups", "dp"), "ctx", None, "head", None),
            P(("groups", "dp"), "ctx", None, "head", None),
            P(("groups", "dp"), "ctx", None, "head", None),
            P(("groups", "dp"), "ctx", None, "head", None),
        ),
        check_vma=False,
    )
```

```python
import functools
import math

import jax
import jax.numpy as jnp
from jax import lax
from jax.experimental import pallas as pl
from jax.experimental.pallas import tpu as pltpu
from jax.sharding import PartitionSpec as P

MESH = pl.DeviceIdType.MESH
F32 = jnp.float32
BF16 = jnp.bfloat16
NT = (((1,), (1,)), ((), ()))
NN = (((1,), (0,)), ((), ()))
TN = (((0,), (0,)), ((), ()))


def mm(a, b, dims):
    return lax.dot_general(a, b, dims, preferred_element_type=F32)


def row_piece(buf, acc, stage, i, b, tokens, depth):
    scaling = 1.0 / math.sqrt(depth)
    block = tokens // 2
    rows = pl.ds(b * block, block)
    span = (b + 1) * block
    q = buf[i, Q, rows]
    g = buf[i, G, rows]
    k = buf[i, K, pl.ds(0, span)]
    v = buf[i, V, pl.ds(0, span)]
    s = mm(q, k, NT) * scaling
    qpos = lax.broadcasted_iota(jnp.int32, (block, span), 0) + b * block
    kpos = lax.broadcasted_iota(jnp.int32, (block, span), 1)
    s = jnp.where(kpos <= qpos, s, -1e30)
    top = jnp.max(s, axis=-1, keepdims=True)
    e = jnp.exp(s - top)
    p = e * (1.0 / jnp.sum(e, axis=-1, keepdims=True))
    pb = p.astype(BF16)
    o = mm(pb, v, NN).astype(BF16)
    dots = jnp.sum(g.astype(F32) * o.astype(F32), axis=-1, keepdims=True)
    dp = mm(g, v, NT)
    ds = (p * (dp - dots) * scaling).astype(BF16)
    stage[i, 0, rows] = o
    stage[i, 1, rows] = mm(ds, k, NN).astype(BF16)
    dk = mm(ds, q, TN)
    dv = mm(pb, g, TN)
    if b == 1:
        acc[0] = dk[:block]
        acc[1] = dv[:block]
        stage[i, 2, rows] = dk[block:].astype(BF16)
        stage[i, 3, rows] = dv[block:].astype(BF16)
    else:
        stage[i, 2, rows] = (acc[0] + dk).astype(BF16)
        stage[i, 3, rows] = (acc[1] + dv).astype(BF16)


def dot(a, b):
    return jnp.sum(a * b, axis=-1, keepdims=True)


def add_up(terms):
    return functools.reduce(jnp.add, terms)


def attend_to(q, g, keys, scaling, rest=None):
    s = [dot(q, k) * scaling for k, _ in keys]
    dp = [dot(g, v) for _, v in keys]
    if rest is not None:
        s, dp = s + [rest[0]], dp + [rest[1]]
    top = functools.reduce(jnp.maximum, s)
    e = [jnp.exp(x - top) for x in s]
    total = add_up(e)
    inverse = 1.0 / total
    p = [x * inverse for x in e]
    dots = add_up([x * y for x, y in zip(p, dp)])
    ds = [x * (y - dots) * scaling for x, y in zip(p, dp)]
    o = add_up([x * kv[1] for x, kv in zip(p, keys)])
    dq = add_up([x * kv[0] for x, kv in zip(ds, keys)])
    return o, dq, p, ds, top + jnp.log(total), dots


def to_rows(columns):
    tokens = columns[0].shape[0]
    lane = lax.broadcasted_iota(jnp.int32, (tokens, 128), 1)
    wide = jnp.broadcast_to(columns[0], (tokens, 128))
    for i, x in enumerate(columns[1:], 1):
        wide = jnp.where(lane == i, x, wide)
    return jnp.transpose(wide)[:8]


def stack_rows(rows):
    index = lax.broadcasted_iota(jnp.int32, (8, rows[0].shape[1]), 0)
    out = jnp.broadcast_to(rows[0], index.shape)
    for i, x in enumerate(rows[1:], 1):
        out = jnp.where(index == i, x, out)
    return out


def to_columns(rows, count):
    turned = jnp.transpose(jnp.concatenate([rows] * 16, axis=0))
    return [turned[:, i : i + 1] for i in range(count)]


Q, G, K, V = 0, 1, 2, 3
QUARTERS = 4
KV0, KV1, QG2, QG3, SC, GA, GB, OD_A, OD_B, SCD = range(10)


def start(copy):
    copy.start()


def received(copy):
    copy.wait_recv()


def gone(copy):
    copy.wait_send()


def each(first, last, body):
    def step(i, _):
        body(i)
        return 0

    lax.fori_loop(first, last, step, 0)


def kernel(
    q_ref, k_ref, v_ref, g_ref, o_out, dq_out, dk_out, dv_out, late,
    fetched, wide, rows_in, cols_in, rows_stage, joined, acc, own_grads,
    kv0, kv1, qg2, qg3, sc, grads_a, grads_b, od_a, od_b, scd,
    sc_stage, scd_stage, send_a, send_b, send_c,
    load, sent, got,
):
    tokens, local_heads, depth = q_ref.shape
    heads = local_heads // 2
    columns = tokens // QUARTERS
    chunks = heads * QUARTERS
    scaling = 1.0 / math.sqrt(depth)
    me = lax.axis_index("ctx")
    refs = (q_ref, g_ref, k_ref, v_ref)
    outs = (o_out, dq_out, dk_out, dv_out)
    shift = jnp.where(me < 2, 1, 0)
    late_quarter = jnp.where(me < 2, QUARTERS - 1, 0)
    late_first = jnp.where(me < 2, 2, 0)

    barrier = pltpu.get_barrier_semaphore()

    def greet(target):
        pl.semaphore_signal(barrier, inc=1, device_id={"ctx": target}, device_id_type=MESH)

    @pl.when(me == 1)
    def _():
        greet(0)
        greet(2)

    @pl.when(me == 2)
    def _():
        greet(1)
        greet(3)

    def turn(step):
        return lax.rem(step + shift, QUARTERS)

    def fetch(at, quarter):
        part = pl.ds(quarter * columns, columns)
        return pltpu.make_async_copy(refs[at].at[part], fetched.at[at, part], load.at[at, quarter])

    def fetch_first(arrays):
        for at in arrays:
            fetch(at, turn(0)).start()

    def fetch_rest(arrays, others):
        for at in others:
            fetch(at, turn(0)).start()

        def later(step):
            for at in arrays + others:
                fetch(at, turn(step)).start()

        each(1, QUARTERS, later)

    @pl.when(me < 2)
    def _():
        fetch_first((K, V))

    @pl.when(me >= 2)
    def _():
        fetch_first((Q, G))

    def remote(src, dst, send, recv, c, slot, target):
        return pltpu.make_async_remote_copy(
            src_ref=src, dst_ref=dst, send_sem=sent.at[send, c], recv_sem=got.at[recv, slot],
            device_id={"ctx": target}, device_id_type=MESH,
        )

    def widen(at, quarter):
        fetch(at, quarter).wait()
        x = fetched[at, pl.ds(quarter * columns, columns)].astype(F32)
        wide[at] = x.reshape(columns * local_heads, depth)

    def take_row(at, quarter, i):
        x = wide[at, pl.ds(2 * i, columns, stride=local_heads)].astype(BF16)
        rows_in[i, at, pl.ds(quarter * columns, columns)] = x

    def take_column(at, quarter, i):
        x = wide[at, pl.ds(2 * i + 1, columns, stride=local_heads)].astype(BF16)
        cols_in[quarter * heads + i, at] = x

    def split(at, quarter):
        widen(at, quarter)
        for i in range(heads):
            take_row(at, quarter, i)
            take_column(at, quarter, i)

    def split_first(arrays, quarter, send, alone, both):
        for at in arrays:
            widen(at, quarter)
        pl.semaphore_wait(barrier, 1)
        for i in range(heads):
            for at in arrays:
                take_column(at, quarter, i)
            if i < alone:
                send(quarter * heads + i, 1).start()
            if i == heads - 1 and alone == 2 and both:
                send(quarter * heads + 2, 2).start()
        for i in range(heads):
            for at in arrays:
                take_row(at, quarter, i)

    def place_rows(quarter):
        part = pl.ds(quarter * columns, columns)
        for a in range(4):
            for h in range(heads):
                x = rows_stage[h, a, part].astype(F32)
                joined[a, quarter, pl.ds(2 * h, columns, stride=local_heads)] = x

        @pl.when(quarter == late_quarter)
        def _():
            for a in range(2):
                for h in range(heads):
                    x = rows_stage[h, late_first + a, part].astype(F32)
                    late[a, pl.ds(2 * h, columns, stride=local_heads)] = x

    def emit_late(c, values):
        for a, x in enumerate(values):
            late[a, pl.ds(2 * (c % heads) + 1, columns, stride=local_heads)] = x

    def emit(c, first, values):
        for a, x in enumerate(values, first):
            spots = pl.ds(2 * (c % heads) + 1, columns, stride=local_heads)
            joined[a, c // heads, spots] = x.astype(F32)

    def join(a, quarter):
        part = pl.ds(quarter * columns, columns)
        outs[a][part] = joined[a, quarter].reshape(columns, local_heads, depth).astype(BF16)

    def vectors(buf, c):
        return [buf[c, a].astype(F32) for a in range(buf.shape[1])]

    def put(ref, c, first, values):
        for a, x in enumerate(values):
            ref[c, first + a] = x.astype(ref.dtype)

    def flow(src, dst, send, recv, target, shift=0):
        def copy(c, n):
            return remote(
                src(pl.ds(c, n)), dst.at[pl.ds(c + shift, n)], send, recv, c, c + shift, target
            )

        return copy

    def whole(buf):
        return lambda part: buf.at[part]

    def halves(first):
        return lambda part: cols_in.at[part, pl.ds(first, 2)]

    kv0_copy = flow(halves(K), kv0, 0, KV0, 1)
    kv0_forward = flow(whole(kv0), kv0, 0, KV0, 2)
    kv1_copy = flow(halves(K), kv1, 1, KV1, 2)
    grads_1_to_0 = flow(whole(send_a), grads_b, 2, GB, 0)
    od_1_to_2 = flow(whole(send_b), od_b, 3, OD_B, 2)
    od3_1_to_2 = flow(whole(send_c), od_b, 4, OD_B, 2, heads)
    scd_1_to_2 = flow(whole(scd_stage), scd, 5, SCD, 2)
    scd_forward = flow(whole(scd), scd, 6, SCD, 3)
    qg2_copy = flow(halves(Q), qg2, 0, QG2, 1)
    qg3_forward = flow(whole(qg3), qg3, 1, QG3, 1)
    sc_2_to_1 = flow(lambda part: sc_stage.at[1, part], sc, 2, SC, 1)
    grads_2_to_0 = flow(whole(send_a), grads_a, 3, GA, 0)
    grads_2_to_1 = flow(whole(send_b), grads_a, 4, GA, 1)
    od_2_to_3 = flow(whole(send_c), od_a, 5, OD_A, 3)
    scd_2_to_3 = flow(whole(scd_stage), scd, 6, SCD, 3)
    qg3_copy = flow(halves(Q), qg3, 0, QG3, 2)
    sc_3_to_2 = flow(lambda part: sc_stage.at[0, part], sc, 1, SC, 2)

    def opening(c):
        return (c >= heads) & (c < heads + 2)

    def lead(c):
        return (c < 2) | opening(c)

    def every(c):
        return c >= 0

    def edge(c):
        return opening(c) | (c >= chunks - 2)

    def at_first(copy, c, act, alone=None):
        if alone is None:
            pl.when(c % 2 == 0)(lambda: act(copy(c, 2)))
        else:
            pl.when(alone(c))(lambda: act(copy(c, 1)))
            pl.when(jnp.logical_not(alone(c)) & (c % 2 == 0))(lambda: act(copy(c, 2)))

    def at_last(copy, c, act, alone=None):
        if alone is None:
            pl.when(c % 2 == 1)(lambda: act(copy(c - 1, 2)))
        else:
            pl.when(alone(c))(lambda: act(copy(c, 1)))
            pl.when(jnp.logical_not(alone(c)) & (c % 2 == 1))(lambda: act(copy(c - 1, 2)))

    @pl.when(me == 0)
    def _():
        split_first((K, V), 1, kv0_copy, heads, True)
        fetch_rest((K, V), (Q, G))

        def go(step):
            quarter = turn(step)

            @pl.when(step > 0)
            def _():
                split(K, quarter)
                split(V, quarter)
                each(0, heads, lambda i: kv0_copy(quarter * heads + i, 1).start())

            split(Q, quarter)
            split(G, quarter)

        each(0, QUARTERS, go)

    @pl.when(me == 1)
    def _():
        split_first((K, V), 1, kv1_copy, 2, False)
        fetch_rest((K, V), (Q, G))

    @pl.when(me == 2)
    def _():
        split_first((Q, G), 0, qg2_copy, 2, True)
        fetch_rest((Q, G), (K, V))
        split(K, 0)
        split(V, 0)

        def pass_on(c):
            at_first(qg3_copy, c, received, every)
            at_last(qg3_forward, c, start, lead)
            q, g, k, v = vectors(cols_in, c)
            q3, g3 = vectors(qg3, c)
            own = to_rows([dot(q, k) * scaling, dot(g, v), dot(q3, k) * scaling, dot(g3, v)])
            sc_stage[0, c] = own

            @pl.when(c < QUARTERS - 1)
            def _():
                for at in range(4):
                    split(at, c + 1)

        each(0, heads, pass_on)

        def merge(c):
            at_first(sc_3_to_2, c, received, every)
            own, far = sc_stage[0, c], sc[c]
            s32, dp32, s33, dp33 = own[2:3], own[3:4], far[0:1], far[1:2]
            top = jnp.maximum(s32, s33)
            e32, e33 = jnp.exp(s32 - top), jnp.exp(s33 - top)
            total = e32 + e33
            mean = (e32 * dp32 + e33 * dp33) / total
            sc_stage[1, c] = stack_rows([own[0:1], own[1:2], top + jnp.log(total), mean])
            at_last(sc_2_to_1, c, start)

        each(0, heads, merge)

    @pl.when(me == 3)
    def _():
        split_first((Q, G), 0, qg3_copy, heads, True)
        fetch_rest((Q, G), (K, V))

        def go(quarter):
            @pl.when(quarter > 0)
            def _():
                split(Q, quarter)
                split(G, quarter)

            split(K, quarter)
            split(V, quarter)

            def scores(i):
                c = quarter * heads + i

                @pl.when(quarter > 0)
                def _():
                    at_first(qg3_copy, c, start, every)

                q, g, k, v = vectors(cols_in, c)
                sc_stage[0, c] = to_rows([dot(q, k) * scaling, dot(g, v)])
                at_last(sc_3_to_2, c, start, every)

            each(0, heads, scores)

        each(0, QUARTERS, go)

    def chunk_0(t):
        c = jnp.where(t < 2 * heads, t + heads, jnp.where(t < 3 * heads, t - 2 * heads, t))
        q, g, k, v = vectors(cols_in, c)
        o, dq, p, ds, _, _ = attend_to(q, g, [(k, v)], scaling)
        emit(c, 0, (o, dq))
        at_first(kv0_copy, c, gone, every)

        @pl.when(t == chunks - 1)
        def _():
            join(0, 3)
            join(1, 3)

        at_first(grads_1_to_0, c, received, every)
        near = vectors(grads_b, c)
        total = (ds[0] * q + near[0], p[0] * g + near[1])

        @pl.when(c < heads)
        def _():
            emit(c, 2, total)

        @pl.when(c >= heads)
        def _():
            at_first(grads_2_to_0, c, received, edge)
            far = vectors(grads_a, c)
            whole = (total[0] + far[0], total[1] + far[1])

            @pl.when(c < chunks - heads)
            def _():
                emit(c, 2, whole)

            @pl.when(c >= chunks - heads)
            def _():
                emit_late(c, whole)

    def chunk_1a(t):
        c = t + heads
        at_first(kv0_copy, c, received, every)
        at_first(kv0_forward, c, start, every)

        @pl.when((t % 2 == 1) & (t <= 5))
        def _():
            split(K, (t // 2 + 2) % QUARTERS)
            split(V, (t // 2 + 2) % QUARTERS)

        @pl.when(c + 2 < chunks)
        def _():
            kv1_copy(c + 2, 1).start()

        @pl.when((t % 2 == 0) & (t <= 6))
        def _():
            split(Q, (t // 2 + 1) % QUARTERS)
            split(G, (t // 2 + 1) % QUARTERS)

        q, g, k, v = vectors(cols_in, c)
        k0, v0 = vectors(kv0, c)
        o, dq, p, ds, _, _ = attend_to(q, g, [(k0, v0), (k, v)], scaling)
        put(send_a, c, 0, (ds[0] * q, p[0] * g))
        at_last(grads_1_to_0, c, start, every)
        emit(c, 0, (o, dq))
        put(own_grads, c, 0, (ds[1] * q, p[1] * g))

    def chunk_1b(c):
        at_first(kv0_copy, c, received, every)
        at_first(qg2_copy, c, received, lead)
        at_first(qg3_forward, c, received, lead)
        at_first(sc_2_to_1, c, received)
        q, g, k, v = vectors(cols_in, c)
        k0, v0 = vectors(kv0, c)
        keys = [(k0, v0), (k, v)]
        rest = to_columns(sc[c], 4)
        q2, g2 = vectors(qg2, c)
        o2, dq2, p2, ds2, lse2, dots2 = attend_to(q2, g2, keys, scaling, rest[:2])
        q3, g3 = vectors(qg3, c)
        o3, dq3, p3, ds3, lse3, dots3 = attend_to(q3, g3, keys, scaling, rest[2:])
        scd_stage[c] = to_rows([lse3, dots3, lse2, dots2])
        at_last(scd_1_to_2, c, start)
        put(send_b, c, 0, (o2, dq2))
        put(send_c, c, 0, (o3, dq3))

        o, dq, p, ds, _, _ = attend_to(q, g, keys, scaling)
        emit(c, 0, (o, dq))
        dk = [ds[j] * q + ds2[j] * q2 + ds3[j] * q3 for j in range(2)]
        dv = [p[j] * g + p2[j] * g2 + p3[j] * g3 for j in range(2)]
        put(send_a, c, 0, (dk[0], dv[0]))
        at_last(grads_1_to_0, c, start, every)
        emit(c, 2, (dk[1], dv[1]))

    def chunk_2a(t):
        c = t + heads
        at_first(kv1_copy, c, received, every)
        at_first(kv0_forward, c, received, every)
        at_first(qg3_copy, c, received, every)
        at_first(sc_3_to_2, c, received, every)
        q, g, k, v = vectors(cols_in, c)
        q3, g3 = vectors(qg3, c)
        k0, v0 = vectors(kv0, c)
        k1, v1 = vectors(kv1, c)
        keys = [(k0, v0), (k1, v1), (k, v)]
        rest = to_columns(sc[c], 2)
        o, dq, p, ds, _, _ = attend_to(q, g, keys, scaling)
        o3, dq3, p3, ds3, lse3, dots3 = attend_to(q3, g3, keys, scaling, rest)
        dk = [ds[j] * q + ds3[j] * q3 for j in range(3)]
        dv = [p[j] * g + p3[j] * g3 for j in range(3)]
        put(send_a, c, 0, (dk[0], dv[0]))
        at_last(grads_2_to_0, c, start, edge)
        put(send_b, c, 0, (dk[1], dv[1]))

        @pl.when(t < 2)
        def _():
            grads_2_to_1(c, 1).start()

        @pl.when(t >= heads)
        def _():
            at_last(grads_2_to_1, c - 2, start)

        @pl.when(t == 3 * heads - 1)
        def _():
            grads_2_to_1(chunks - 2, 2).start()

        scd_stage[c] = to_rows([lse3, dots3])
        at_last(scd_2_to_3, c, start, every)
        put(send_c, c, 0, (o3, dq3))
        at_last(od_2_to_3, c, start, every)
        emit(c, 0, (o, dq, dk[2], dv[2]))

    def chunk_2b(c):
        at_first(scd_1_to_2, c, received)
        at_first(scd_forward, c, start, every)
        own, far = sc_stage[0, c], scd[c]
        p3 = jnp.exp(own[2:3] - far[0:1])
        ds3 = p3 * (own[3:4] - far[1:2]) * scaling
        p2 = jnp.exp(own[0:1] - far[2:3])
        ds2 = p2 * (own[1:2] - far[3:4]) * scaling
        p3, ds3, p2, ds2 = to_columns(stack_rows([p3, ds3, p2, ds2]), 4)
        q, g, k, v = vectors(cols_in, c)
        put(own_grads, c + heads, 0, (p3 * v, ds3 * k))
        q3, g3 = vectors(qg3, c)
        emit(c, 2, (ds2 * q + ds3 * q3, p2 * g + p3 * g3))
        put(own_grads, c, 0, (p2 * v, ds2 * k))

    def pass_on_od3(c):
        od3_1_to_2(c, 1).wait_recv()
        far = vectors(od_b, c + heads)
        put(send_c, c, 0, [own_grads[c + heads, a] + far[a] for a in range(2)])
        at_last(od_2_to_3, c, start, every)

    def finish_2(c):
        at_first(qg2_copy, c, gone, lead)
        at_first(qg3_forward, c, gone, lead)
        at_first(sc_2_to_1, c, gone)

        def done(late):
            at_first(grads_2_to_0, late, gone, edge)
            at_first(grads_2_to_1, late, gone, opening)
            at_first(scd_2_to_3, late, gone, every)
            at_first(od_2_to_3, late, gone, every)

        each(heads + 3 * c, heads + 3 * c + 3, done)
        at_first(scd_forward, c, gone, every)
        at_first(od_2_to_3, c, gone, every)

        @pl.when(c > 0)
        def _():
            for a in range(4):
                join(a, c)

        @pl.when(c == 0)
        def _():
            join(2, 0)
            join(3, 0)

        od_1_to_2(c, 1).wait_recv()
        far = vectors(od_b, c)
        emit_late(c, [own_grads[c, a] + far[a] for a in range(2)])

    def chunk_3(c):
        at_first(scd_2_to_3, c, received, every)
        own, far = sc_stage[0, c], scd[c]
        p = jnp.exp(own[0:1] - far[0:1])
        ds = p * (own[1:2] - far[1:2]) * scaling
        p, ds = to_columns(stack_rows([p, ds]), 2)
        q, g, k, v = vectors(cols_in, c)
        emit(c, 2, (ds * q, p * g))
        at_first(qg3_copy, c, gone, every)
        at_first(sc_3_to_2, c, gone, every)
        own = (p * v, ds * k)

        @pl.when(c >= heads)
        def _():
            at_first(od_2_to_3, c, received, every)
            near = vectors(od_a, c)
            emit(c, 0, (own[0] + near[0], own[1] + near[1]))

        @pl.when(c < heads)
        def _():
            put(own_grads, c, 0, own)

    def finish_3(c):
        at_first(od_2_to_3, c, received, every)
        far = vectors(od_a, c)
        emit_late(c, [own_grads[c, a] + far[a] for a in range(2)])

    ends = (me == 0) | (me == 3)
    first_row = jnp.where(me == 1, 3 * heads, jnp.where(me == 2, 1, -3 * heads))
    first_step = jnp.where(ends, -3 * heads, 0)
    steps = jnp.where(me == 1, chunks + 2 * heads, chunks)

    def body(t):
        piece = t - first_row
        here = (piece >= 0) & (piece < 2 * heads)

        @pl.when(here & (piece % 2 == 0))
        def _():
            row_piece(rows_in, acc, rows_stage, piece // 2, 1, tokens, depth)

        @pl.when(here & (piece % 2 == 1))
        def _():
            row_piece(rows_in, acc, rows_stage, piece // 2, 0, tokens, depth)

        rest = piece - 2 * heads

        @pl.when((rest >= 0) & (rest < QUARTERS))
        def _():
            place_rows(rest)

        @pl.when(ends & ((t == heads) | (t == 2 * heads) | (t == 3 * heads)))
        def _():
            quarter = jnp.where((me == 0) & (t == 3 * heads), 0, t // heads)
            for a in range(4):
                join(a, quarter)

        @pl.when((me == 0) & (t >= 0))
        def _():
            chunk_0(t)

        @pl.when((me == 1) & (t >= 0) & (t < 3 * heads))
        def _():
            chunk_1a(t)

        @pl.when((me == 1) & (t >= FIRST_B) & (t < FIRST_B + heads))
        def _():
            chunk_1b(t - FIRST_B)

        @pl.when((me == 1) & (t == 3 * heads - 1))
        def _():
            each(0, heads, lambda c: od3_1_to_2(c, 1).start())
            each(0, heads, lambda c: od_1_to_2(c, 1).start())

        @pl.when((me == 2) & (t < 3 * heads))
        def _():
            chunk_2a(t)

        @pl.when((me == 2) & (t >= 2 * heads) & (t < 3 * heads))
        def _():
            chunk_2b(t - 2 * heads)

        @pl.when((me == 3) & (t >= 0))
        def _():
            @pl.when(t < 3 * heads)
            def _():
                chunk_3(t + heads)

            @pl.when((t >= 2 * heads) & (t < 3 * heads))
            def _():
                chunk_3(t - 2 * heads)

    each(first_step, steps, body)

    @pl.when(me == 1)
    def _():
        join(2, 0)
        join(3, 0)

        def join_early(quarter):
            join(0, quarter)
            join(1, quarter)

        each(0, QUARTERS, join_early)

        def finish(c):
            at_first(kv0_forward, c, gone, every)
            at_first(kv1_copy, c, gone, every)
            at_first(grads_1_to_0, c, gone, every)

            @pl.when(c == chunks - 2)
            def _():
                each(0, heads, done_b)

            at_first(grads_2_to_1, c, received, opening)
            far = vectors(grads_a, c)
            total = [own_grads[c, a] + far[a] for a in range(2)]

            @pl.when(c < chunks - heads)
            def _():
                emit(c, 2, total)

            @pl.when(c >= chunks - heads)
            def _():
                emit_late(c, total)

            @pl.when((c % heads == heads - 1) & (c < chunks - 1))
            def _():
                join(2, c // heads)
                join(3, c // heads)

        def done_b(c):
            at_first(grads_1_to_0, c, gone, every)
            at_first(scd_1_to_2, c, gone)
            od3_1_to_2(c, 1).wait_send()
            od_1_to_2(c, 1).wait_send()

        each(heads, chunks, finish)

    @pl.when(me == 3)
    def _():
        join(2, 0)
        join(3, 0)
        each(0, heads, finish_3)

    @pl.when(me == 2)
    def _():
        each(0, heads, pass_on_od3)
        each(0, heads, finish_2)


FIRST_B = 7


def store_kernel(*refs):
    ins, late, outs, last, leave = refs[:4], refs[4], refs[5:9], refs[9], refs[10]
    tokens, local_heads, depth = ins[0].shape
    columns = tokens // QUARTERS
    me = lax.axis_index("ctx")

    def send(a, first, count):
        part = pl.ds(first * columns, count * columns)
        return pltpu.make_async_copy(ins[a].at[part], outs[a].at[part], leave.at[a])

    def send_last(a, quarter):
        part = pl.ds(quarter * columns, columns)
        return pltpu.make_async_copy(last.at[a % 2], outs[a].at[part], leave.at[4 + a % 2])

    def store(arrays, others, first, quarter):
        whole = [send(a, 0, QUARTERS) for a in others] + [send(a, first, QUARTERS - 1) for a in arrays]
        for copy in whole:
            copy.start()
        for i, a in enumerate(arrays):
            last[i] = late[i].reshape(columns, local_heads, depth).astype(BF16)
            send_last(a, quarter).start()
        for copy in whole:
            copy.wait()
        for a in arrays:
            send_last(a, quarter).wait()

    @pl.when(me < 2)
    def _():
        store((2, 3), (0, 1), 0, QUARTERS - 1)

    @pl.when(me >= 2)
    def _():
        store((0, 1), (2, 3), 1, 0)


def fused(queries, key_vecs, value_vecs, grad_out):
    shape = queries.shape
    tokens, local_heads, depth = shape[2:]
    heads = local_heads // 2
    columns = tokens // QUARTERS
    chunks = heads * QUARTERS
    flat = [
        pltpu.with_memory_space_constraint(x.reshape(tokens, local_heads, depth), pltpu.HBM)
        for x in (queries, key_vecs, value_vecs, grad_out)
    ]
    hbm = pl.BlockSpec(memory_space=pltpu.HBM)
    vmem = pl.BlockSpec(memory_space=pltpu.VMEM)
    two = pltpu.VMEM((chunks, 2, columns, depth), BF16)
    few = pltpu.VMEM((heads, 2, columns, depth), BF16)
    four = pltpu.VMEM((chunks, 4, columns, depth), BF16)
    row_buf = pltpu.VMEM((heads, 4, tokens, depth), BF16)
    flat_rows = pltpu.VMEM((chunks, 8, columns), F32)
    dma = pltpu.SemaphoreType.DMA
    parts = pl.pallas_call(
        kernel,
        out_shape=[pltpu.VMEM((tokens, local_heads, depth), BF16)] * 4
        + [pltpu.VMEM((2, columns * local_heads, depth), F32)],
        in_specs=[hbm] * 4,
        out_specs=[vmem] * 5,
        scratch_shapes=[
            pltpu.VMEM((4, tokens, local_heads, depth), BF16),
            pltpu.VMEM((4, columns * local_heads, depth), F32),
            row_buf, four, row_buf,
            pltpu.VMEM((4, QUARTERS, columns * local_heads, depth), F32),
            pltpu.VMEM((2, tokens // 2, depth), F32),
            pltpu.VMEM((chunks, 2, columns, depth), F32),
            two, two, few, two, flat_rows, two, two, two, two, flat_rows,
            pltpu.VMEM((2, chunks, 8, columns), F32), flat_rows,
            two, two, two,
            dma((4, QUARTERS)), dma((7, chunks)), dma((10, chunks)),
        ],
        compiler_params=pltpu.CompilerParams(
            collective_id=0, has_side_effects=True, vmem_limit_bytes=44 * 1024 * 1024
        ),
    )(*flat)
    results = pl.pallas_call(
        store_kernel,
        out_shape=[jax.ShapeDtypeStruct((tokens, local_heads, depth), BF16)] * 4,
        in_specs=[vmem] * 5,
        out_specs=[pl.BlockSpec(memory_space=pl.ANY)] * 4,
        scratch_shapes=[pltpu.VMEM((2, columns, local_heads, depth), BF16), dma((6,))],
        compiler_params=pltpu.CompilerParams(vmem_limit_bytes=2 * 1024 * 1024),
    )(*parts)
    return tuple(x.reshape(shape) for x in results)


def causal(length):
    positions = jnp.arange(length)
    return positions[None, :] <= positions[:, None]


def attend(query_in, key_in, value_in, grad_in, layout, allowed):
    scaling = 1.0 / math.sqrt(query_in.shape[-1])
    key_form = layout.replace("q", "k")
    scores = (
        jnp.einsum(
            layout + "," + key_form + "->bxhqk",
            query_in,
            key_in,
            preferred_element_type=jnp.float32,
        )
        * scaling
    )
    scores = jnp.where(allowed, scores, -1e30)
    highest = jnp.max(scores, axis=-1, keepdims=True)
    weight_sum = jnp.sum(jnp.exp(scores - highest), axis=-1, keepdims=True)
    log_total = highest + jnp.log(weight_sum)
    weights = jnp.where(allowed, jnp.exp(scores - log_total), 0.0)
    rounded = weights.astype(jnp.bfloat16)
    output = jnp.einsum(
        "bxhqk," + key_form + "->" + layout, rounded, value_in, preferred_element_type=jnp.float32
    ).astype(jnp.bfloat16)
    row_dots = jnp.einsum(
        layout + "," + layout + "->bxhq", grad_in, output, preferred_element_type=jnp.float32
    )
    dprobs = jnp.einsum(
        layout + "," + key_form + "->bxhqk", grad_in, value_in, preferred_element_type=jnp.float32
    )
    dscores = (weights * (dprobs - row_dots[..., None]) * scaling).astype(jnp.bfloat16)
    grad_query = jnp.einsum(
        "bxhqk," + key_form + "->" + layout, dscores, key_in, preferred_element_type=jnp.float32
    ).astype(jnp.bfloat16)
    grad_key = jnp.einsum(
        "bxhqk," + layout + "->" + key_form, dscores, query_in, preferred_element_type=jnp.float32
    )
    grad_value = jnp.einsum(
        "bxhqk," + layout + "->" + key_form, rounded, grad_in, preferred_element_type=jnp.float32
    )
    return (output, grad_query, grad_key, grad_value)


def merge_heads(first_part, second_part):
    stacked = jnp.stack((first_part, second_part), axis=4)
    shape = first_part.shape
    return stacked.reshape(shape[:3] + (2 * shape[3], shape[4]))


def per_device(queries, key_vecs, value_vecs, grad_out):
    arrays = (queries, key_vecs, value_vecs, grad_out)
    row_parts = tuple((array[:, :, :, 0::2] for array in arrays))
    col_parts = tuple((array[:, :, :, 1::2] for array in arrays))
    row_local = attend(
        row_parts[0], row_parts[1], row_parts[2], row_parts[3], "bxqhd", causal(queries.shape[2])
    )
    row_results = (
        row_local[0],
        row_local[1],
        row_local[2].astype(jnp.bfloat16),
        row_local[3].astype(jnp.bfloat16),
    )
    local_rows = col_parts[0].shape[1]
    gathered = (
        lax.all_gather(col_parts[1], "ctx", axis=1, tiled=True),
        lax.all_gather(col_parts[2], "ctx", axis=1, tiled=True),
    )
    query_rows = lax.axis_index("ctx") * local_rows + jnp.arange(local_rows)
    key_rows = jnp.arange(gathered[0].shape[1])
    allowed = key_rows[None, :] <= query_rows[:, None]
    col_local = attend(col_parts[0], gathered[0], gathered[1], col_parts[3], "bqxhd", allowed)
    summed = (
        lax.psum_scatter(col_local[2], "ctx", scatter_dimension=1, tiled=True),
        lax.psum_scatter(col_local[3], "ctx", scatter_dimension=1, tiled=True),
    )
    col_results = (
        col_local[0],
        col_local[1],
        summed[0].astype(jnp.bfloat16),
        summed[1].astype(jnp.bfloat16),
    )
    return (
        merge_heads(row_results[0], col_results[0]),
        merge_heads(row_results[1], col_results[1]),
        merge_heads(row_results[2], col_results[2]),
        merge_heads(row_results[3], col_results[3]),
    )


def solution(mesh):
    body = fused if mesh.shape["ctx"] == 4 else per_device
    placed = (
        P(("groups", "dp"), "ctx", None, "head", None),
        P(("groups", "dp"), "ctx", None, "head", None),
        P(("groups", "dp"), "ctx", None, "head", None),
        P(("groups", "dp"), "ctx", None, "head", None),
    )
    return jax.shard_map(
        body,
        mesh=mesh,
        in_specs=placed,
        out_specs=(
            P(("groups", "dp"), "ctx", None, "head", None),
            P(("groups", "dp"), "ctx", None, "head", None),
            P(("groups", "dp"), "ctx", None, "head", None),
            P(("groups", "dp"), "ctx", None, "head", None),
        ),
        check_vma=False,
    )
```

```python
import functools
import math

import jax
import jax.numpy as jnp
from jax import lax
from jax.experimental import pallas as pl
from jax.experimental.pallas import tpu as pltpu
from jax.sharding import PartitionSpec as P

MESH = pl.DeviceIdType.MESH
F32 = jnp.float32
BF16 = jnp.bfloat16
NT = (((1,), (1,)), ((), ()))
NN = (((1,), (0,)), ((), ()))
TN = (((0,), (0,)), ((), ()))


def mm(a, b, dims):
    return lax.dot_general(a, b, dims, preferred_element_type=F32)


def row_piece(buf, acc, stage, i, b, tokens, depth):
    scaling = 1.0 / math.sqrt(depth)
    block = tokens // 2
    rows = pl.ds(b * block, block)
    span = (b + 1) * block
    q = buf[i, Q, rows]
    g = buf[i, G, rows]
    k = buf[i, K, pl.ds(0, span)]
    v = buf[i, V, pl.ds(0, span)]
    s = mm(q, k, NT) * scaling
    qpos = lax.broadcasted_iota(jnp.int32, (block, span), 0) + b * block
    kpos = lax.broadcasted_iota(jnp.int32, (block, span), 1)
    s = jnp.where(kpos <= qpos, s, -1e30)
    top = jnp.max(s, axis=-1, keepdims=True)
    e = jnp.exp(s - top)
    p = e * (1.0 / jnp.sum(e, axis=-1, keepdims=True))
    pb = p.astype(BF16)
    o = mm(pb, v, NN).astype(BF16)
    dots = jnp.sum(g.astype(F32) * o.astype(F32), axis=-1, keepdims=True)
    dp = mm(g, v, NT)
    ds = (p * (dp - dots) * scaling).astype(BF16)
    stage[i, 0, rows] = o
    stage[i, 1, rows] = mm(ds, k, NN).astype(BF16)
    dk = mm(ds, q, TN)
    dv = mm(pb, g, TN)
    if b == 1:
        acc[0] = dk[:block]
        acc[1] = dv[:block]
        stage[i, 2, rows] = dk[block:].astype(BF16)
        stage[i, 3, rows] = dv[block:].astype(BF16)
    else:
        stage[i, 2, rows] = (acc[0] + dk).astype(BF16)
        stage[i, 3, rows] = (acc[1] + dv).astype(BF16)


def dot(a, b):
    return jnp.sum(a * b, axis=-1, keepdims=True)


def add_up(terms):
    return functools.reduce(jnp.add, terms)


def attend_to(q, g, keys, scaling, rest=None):
    s = [dot(q, k) * scaling for k, _ in keys]
    dp = [dot(g, v) for _, v in keys]
    if rest is not None:
        s, dp = s + [rest[0]], dp + [rest[1]]
    top = functools.reduce(jnp.maximum, s)
    e = [jnp.exp(x - top) for x in s]
    total = add_up(e)
    inverse = 1.0 / total
    p = [x * inverse for x in e]
    dots = add_up([x * y for x, y in zip(p, dp)])
    ds = [x * (y - dots) * scaling for x, y in zip(p, dp)]
    o = add_up([x * kv[1] for x, kv in zip(p, keys)])
    dq = add_up([x * kv[0] for x, kv in zip(ds, keys)])
    return o, dq, p, ds, top + jnp.log(total), dots


def to_rows(columns):
    tokens = columns[0].shape[0]
    lane = lax.broadcasted_iota(jnp.int32, (tokens, 128), 1)
    wide = jnp.broadcast_to(columns[0], (tokens, 128))
    for i, x in enumerate(columns[1:], 1):
        wide = jnp.where(lane == i, x, wide)
    return jnp.transpose(wide)[:8]


def stack_rows(rows):
    index = lax.broadcasted_iota(jnp.int32, (8, rows[0].shape[1]), 0)
    out = jnp.broadcast_to(rows[0], index.shape)
    for i, x in enumerate(rows[1:], 1):
        out = jnp.where(index == i, x, out)
    return out


def to_columns(rows, count):
    turned = jnp.transpose(jnp.concatenate([rows] * 16, axis=0))
    return [turned[:, i : i + 1] for i in range(count)]


Q, G, K, V = 0, 1, 2, 3
QUARTERS = 4
KV0, KV1, QG2, QG3, SC, GA, GB, OD_A, OD_B, SCD = range(10)


def start(copy):
    copy.start()


def received(copy):
    copy.wait_recv()


def gone(copy):
    copy.wait_send()


def each(first, last, body):
    def step(i, _):
        body(i)
        return 0

    lax.fori_loop(first, last, step, 0)


def kernel(
    q_ref, k_ref, v_ref, g_ref, o_out, dq_out, dk_out, dv_out, late,
    fetched, wide, rows_in, cols_in, rows_stage, joined, acc, own_grads,
    kv0, kv1, qg2, qg3, sc, grads_a, grads_b, od_a, od_b, scd,
    sc_stage, scd_stage, send_a, send_b, send_c,
    load, sent, got,
):
    tokens, local_heads, depth = q_ref.shape
    heads = local_heads // 2
    columns = tokens // QUARTERS
    chunks = heads * QUARTERS
    scaling = 1.0 / math.sqrt(depth)
    me = lax.axis_index("ctx")
    core = lax.axis_index("dp")
    refs = (q_ref, g_ref, k_ref, v_ref)
    outs = (o_out, dq_out, dk_out, dv_out)
    shift = jnp.where(me < 2, 1, 0)
    late_quarter = jnp.where(me < 2, QUARTERS - 1, 0)
    late_first = jnp.where(me < 2, 2, 0)

    barrier = pltpu.get_barrier_semaphore()

    def greet(target):
        pl.semaphore_signal(barrier, inc=1, device_id={"ctx": target}, device_id_type=MESH)

    @pl.when(me == 1)
    def _():
        greet(0)
        greet(2)

    @pl.when(me == 2)
    def _():
        greet(1)
        greet(3)

    def turn(step):
        return lax.rem(step + shift, QUARTERS)

    def fetch(at, quarter):
        part = pl.ds(quarter * columns, columns)
        return pltpu.make_async_copy(refs[at].at[part], fetched.at[at, part], load.at[at, quarter])

    def fetch_first(arrays):
        for at in arrays:
            fetch(at, turn(0)).start()

    def fetch_rest(arrays, others):
        for at in others:
            fetch(at, turn(0)).start()

        def later(step):
            for at in arrays + others:
                fetch(at, turn(step)).start()

        each(1, QUARTERS, later)

    @pl.when(me < 2)
    def _():
        fetch_first((K, V))

    @pl.when(me >= 2)
    def _():
        fetch_first((Q, G))

    def remote(src, dst, send, recv, c, slot, target):
        return pltpu.make_async_remote_copy(
            src_ref=src, dst_ref=dst, send_sem=sent.at[send, c], recv_sem=got.at[recv, slot],
            device_id={"ctx": target}, device_id_type=MESH,
        )

    def widen(at, quarter):
        fetch(at, quarter).wait()
        x = fetched[at, pl.ds(quarter * columns, columns)].astype(F32)
        wide[at] = x.reshape(columns * local_heads, depth)

    def take_row(at, quarter, i):
        x = wide[at, pl.ds(2 * i, columns, stride=local_heads)].astype(BF16)
        rows_in[i, at, pl.ds(quarter * columns, columns)] = x

    def take_column(at, quarter, i):
        x = wide[at, pl.ds(2 * i + 1, columns, stride=local_heads)].astype(BF16)
        cols_in[quarter * heads + i, at] = x

    def split(at, quarter):
        widen(at, quarter)
        for i in range(heads):
            take_row(at, quarter, i)
            take_column(at, quarter, i)

    def split_first(arrays, quarter, send, alone, both):
        for at in arrays:
            widen(at, quarter)
        pl.semaphore_wait(barrier, 1)
        for i in range(heads):
            for at in arrays:
                take_column(at, quarter, i)
            if i < alone:
                send(quarter * heads + i, 1).start()
            if i == heads - 1 and alone == 2 and both:
                send(quarter * heads + 2, 2).start()
        for i in range(heads):
            for at in arrays:
                take_row(at, quarter, i)

    def place_rows(quarter):
        part = pl.ds(quarter * columns, columns)
        for a in range(4):
            for h in range(heads):
                x = rows_stage[h, a, part].astype(F32)
                joined[a, quarter, pl.ds(2 * h, columns, stride=local_heads)] = x

        @pl.when(quarter == late_quarter)
        def _():
            for a in range(2):
                for h in range(heads):
                    x = rows_stage[h, late_first + a, part].astype(F32)
                    late[a, pl.ds(2 * h, columns, stride=local_heads)] = x

    def emit_late(c, values):
        for a, x in enumerate(values):
            late[a, pl.ds(2 * (c % heads) + 1, columns, stride=local_heads)] = x

    def emit(c, first, values):
        for a, x in enumerate(values, first):
            spots = pl.ds(2 * (c % heads) + 1, columns, stride=local_heads)
            joined[a, c // heads, spots] = x.astype(F32)

    def join(a, quarter):
        part = pl.ds(quarter * columns, columns)
        outs[a][part] = joined[a, quarter].reshape(columns, local_heads, depth).astype(BF16)

    def vectors(buf, c):
        return [buf[c, a].astype(F32) for a in range(buf.shape[1])]

    def put(ref, c, first, values):
        for a, x in enumerate(values):
            ref[c, first + a] = x.astype(ref.dtype)

    def flow(src, dst, send, recv, target, shift=0):
        def copy(c, n):
            return remote(
                src(pl.ds(c, n)), dst.at[pl.ds(c + shift, n)], send, recv, c, c + shift, target
            )

        return copy

    def whole(buf):
        return lambda part: buf.at[part]

    def halves(first):
        return lambda part: cols_in.at[part, pl.ds(first, 2)]

    kv0_copy = flow(halves(K), kv0, 0, KV0, 1)
    kv0_forward = flow(whole(kv0), kv0, 0, KV0, 2)
    kv1_copy = flow(halves(K), kv1, 1, KV1, 2)
    grads_1_to_0 = flow(whole(send_a), grads_b, 2, GB, 0)
    od_1_to_2 = flow(whole(send_b), od_b, 3, OD_B, 2)
    od3_1_to_2 = flow(whole(send_c), od_b, 4, OD_B, 2, heads)
    scd_1_to_2 = flow(whole(scd_stage), scd, 5, SCD, 2)
    scd_forward = flow(whole(scd), scd, 6, SCD, 3)
    qg2_copy = flow(halves(Q), qg2, 0, QG2, 1)
    qg3_forward = flow(whole(qg3), qg3, 1, QG3, 1)
    sc_2_to_1 = flow(lambda part: sc_stage.at[1, part], sc, 2, SC, 1)
    grads_2_to_0 = flow(whole(send_a), grads_a, 3, GA, 0)
    grads_2_to_1 = flow(whole(send_b), grads_a, 4, GA, 1)
    od_2_to_3 = flow(whole(send_c), od_a, 5, OD_A, 3)
    scd_2_to_3 = flow(whole(scd_stage), scd, 6, SCD, 3)
    qg3_copy = flow(halves(Q), qg3, 0, QG3, 2)
    sc_3_to_2 = flow(lambda part: sc_stage.at[0, part], sc, 1, SC, 2)

    def opening(c):
        return (c >= heads) & (c < heads + 2)

    def lead(c):
        return (c < 2) | opening(c)

    def every(c):
        return c >= 0

    def edge(c):
        return opening(c) | (c >= chunks - 2)

    def at_first(copy, c, act, alone=None):
        if alone is None:
            pl.when(c % 2 == 0)(lambda: act(copy(c, 2)))
        else:
            pl.when(alone(c))(lambda: act(copy(c, 1)))
            pl.when(jnp.logical_not(alone(c)) & (c % 2 == 0))(lambda: act(copy(c, 2)))

    def at_last(copy, c, act, alone=None):
        if alone is None:
            pl.when(c % 2 == 1)(lambda: act(copy(c - 1, 2)))
        else:
            pl.when(alone(c))(lambda: act(copy(c, 1)))
            pl.when(jnp.logical_not(alone(c)) & (c % 2 == 1))(lambda: act(copy(c - 1, 2)))

    @pl.when(me == 0)
    def _():
        split_first((K, V), 1, kv0_copy, heads, True)
        fetch_rest((K, V), (Q, G))

        def go(step):
            quarter = turn(step)

            @pl.when(step > 0)
            def _():
                split(K, quarter)
                split(V, quarter)
                each(0, heads, lambda i: kv0_copy(quarter * heads + i, 1).start())

            split(Q, quarter)
            split(G, quarter)

        each(0, QUARTERS, go)

    @pl.when(me == 1)
    def _():
        split_first((K, V), 1, kv1_copy, 2, False)
        fetch_rest((K, V), (Q, G))

    @pl.when(me == 2)
    def _():
        split_first((Q, G), 0, qg2_copy, 2, True)
        fetch_rest((Q, G), (K, V))
        split(K, 0)
        split(V, 0)

        def pass_on(c):
            at_first(qg3_copy, c, received, every)
            at_last(qg3_forward, c, start, lead)
            q, g, k, v = vectors(cols_in, c)
            q3, g3 = vectors(qg3, c)
            own = to_rows([dot(q, k) * scaling, dot(g, v), dot(q3, k) * scaling, dot(g3, v)])
            sc_stage[0, c] = own

            @pl.when(c < QUARTERS - 1)
            def _():
                for at in range(4):
                    split(at, c + 1)

        each(0, heads, pass_on)

        def merge(c):
            at_first(sc_3_to_2, c, received, every)
            own, far = sc_stage[0, c], sc[c]
            s32, dp32, s33, dp33 = own[2:3], own[3:4], far[0:1], far[1:2]
            top = jnp.maximum(s32, s33)
            e32, e33 = jnp.exp(s32 - top), jnp.exp(s33 - top)
            total = e32 + e33
            mean = (e32 * dp32 + e33 * dp33) / total
            sc_stage[1, c] = stack_rows([own[0:1], own[1:2], top + jnp.log(total), mean])
            at_last(sc_2_to_1, c, start)

        each(0, heads, merge)

    @pl.when(me == 3)
    def _():
        split_first((Q, G), 0, qg3_copy, heads, True)
        fetch_rest((Q, G), (K, V))

        def go(quarter):
            @pl.when(quarter > 0)
            def _():
                split(Q, quarter)
                split(G, quarter)

            split(K, quarter)
            split(V, quarter)

            def scores(i):
                c = quarter * heads + i

                @pl.when(quarter > 0)
                def _():
                    at_first(qg3_copy, c, start, every)

                q, g, k, v = vectors(cols_in, c)
                sc_stage[0, c] = to_rows([dot(q, k) * scaling, dot(g, v)])
                at_last(sc_3_to_2, c, start, every)

            each(0, heads, scores)

        each(0, QUARTERS, go)

    def chunk_0(t):
        c = jnp.where(t < 2 * heads, t + heads, jnp.where(t < 3 * heads, t - 2 * heads, t))
        q, g, k, v = vectors(cols_in, c)
        o, dq, p, ds, _, _ = attend_to(q, g, [(k, v)], scaling)
        emit(c, 0, (o, dq))
        at_first(kv0_copy, c, gone, every)

        @pl.when(t == chunks - 1)
        def _():
            join(0, 3)
            join(1, 3)

        at_first(grads_1_to_0, c, received, every)
        near = vectors(grads_b, c)
        total = (ds[0] * q + near[0], p[0] * g + near[1])

        @pl.when(c < heads)
        def _():
            emit(c, 2, total)

        @pl.when(c >= heads)
        def _():
            at_first(grads_2_to_0, c, received, edge)
            far = vectors(grads_a, c)
            whole = (total[0] + far[0], total[1] + far[1])

            @pl.when(c < chunks - heads)
            def _():
                emit(c, 2, whole)

            @pl.when(c >= chunks - heads)
            def _():
                emit_late(c, whole)

    def chunk_1a(t):
        c = t + heads
        at_first(kv0_copy, c, received, every)
        at_first(kv0_forward, c, start, every)

        @pl.when((t % 2 == 1) & (t <= 5))
        def _():
            split(K, (t // 2 + 2) % QUARTERS)
            split(V, (t // 2 + 2) % QUARTERS)

        @pl.when(c + 2 < chunks)
        def _():
            kv1_copy(c + 2, 1).start()

        @pl.when((t % 2 == 0) & (t <= 6))
        def _():
            split(Q, (t // 2 + 1) % QUARTERS)
            split(G, (t // 2 + 1) % QUARTERS)

        q, g, k, v = vectors(cols_in, c)
        k0, v0 = vectors(kv0, c)
        o, dq, p, ds, _, _ = attend_to(q, g, [(k0, v0), (k, v)], scaling)
        put(send_a, c, 0, (ds[0] * q, p[0] * g))
        at_last(grads_1_to_0, c, start, every)
        emit(c, 0, (o, dq))
        put(own_grads, c, 0, (ds[1] * q, p[1] * g))

    def chunk_1b(c):
        at_first(kv0_copy, c, received, every)
        at_first(qg2_copy, c, received, lead)
        at_first(qg3_forward, c, received, lead)
        at_first(sc_2_to_1, c, received)
        q, g, k, v = vectors(cols_in, c)
        k0, v0 = vectors(kv0, c)
        keys = [(k0, v0), (k, v)]
        rest = to_columns(sc[c], 4)
        q2, g2 = vectors(qg2, c)
        o2, dq2, p2, ds2, lse2, dots2 = attend_to(q2, g2, keys, scaling, rest[:2])
        q3, g3 = vectors(qg3, c)
        o3, dq3, p3, ds3, lse3, dots3 = attend_to(q3, g3, keys, scaling, rest[2:])
        scd_stage[c] = to_rows([lse3, dots3, lse2, dots2])
        at_last(scd_1_to_2, c, start)
        put(send_b, c, 0, (o2, dq2))
        put(send_c, c, 0, (o3, dq3))

        o, dq, p, ds, _, _ = attend_to(q, g, keys, scaling)
        emit(c, 0, (o, dq))
        dk = [ds[j] * q + ds2[j] * q2 + ds3[j] * q3 for j in range(2)]
        dv = [p[j] * g + p2[j] * g2 + p3[j] * g3 for j in range(2)]
        put(send_a, c, 0, (dk[0], dv[0]))
        at_last(grads_1_to_0, c, start, every)
        emit(c, 2, (dk[1], dv[1]))

    def chunk_2a(t):
        c = t + heads
        at_first(kv1_copy, c, received, every)
        at_first(kv0_forward, c, received, every)
        at_first(qg3_copy, c, received, every)
        at_first(sc_3_to_2, c, received, every)
        q, g, k, v = vectors(cols_in, c)
        q3, g3 = vectors(qg3, c)
        k0, v0 = vectors(kv0, c)
        k1, v1 = vectors(kv1, c)
        keys = [(k0, v0), (k1, v1), (k, v)]
        rest = to_columns(sc[c], 2)
        o, dq, p, ds, _, _ = attend_to(q, g, keys, scaling)
        o3, dq3, p3, ds3, lse3, dots3 = attend_to(q3, g3, keys, scaling, rest)
        dk = [ds[j] * q + ds3[j] * q3 for j in range(3)]
        dv = [p[j] * g + p3[j] * g3 for j in range(3)]
        put(send_a, c, 0, (dk[0], dv[0]))
        at_last(grads_2_to_0, c, start, edge)
        put(send_b, c, 0, (dk[1], dv[1]))

        @pl.when(core > 0)
        def _():
            at_last(grads_2_to_1, c, start, opening)

        @pl.when((core == 0) & (t < 2))
        def _():
            grads_2_to_1(c, 1).start()

        @pl.when((core == 0) & (t >= heads))
        def _():
            at_last(grads_2_to_1, c - 2, start)

        @pl.when((core == 0) & (t == 3 * heads - 1))
        def _():
            grads_2_to_1(chunks - 2, 2).start()

        scd_stage[c] = to_rows([lse3, dots3])
        at_last(scd_2_to_3, c, start, every)
        put(send_c, c, 0, (o3, dq3))
        at_last(od_2_to_3, c, start, every)
        emit(c, 0, (o, dq, dk[2], dv[2]))

    def chunk_2b(c):
        at_first(scd_1_to_2, c, received)
        at_first(scd_forward, c, start, every)
        own, far = sc_stage[0, c], scd[c]
        p3 = jnp.exp(own[2:3] - far[0:1])
        ds3 = p3 * (own[3:4] - far[1:2]) * scaling
        p2 = jnp.exp(own[0:1] - far[2:3])
        ds2 = p2 * (own[1:2] - far[3:4]) * scaling
        p3, ds3, p2, ds2 = to_columns(stack_rows([p3, ds3, p2, ds2]), 4)
        q, g, k, v = vectors(cols_in, c)
        put(own_grads, c + heads, 0, (p3 * v, ds3 * k))
        q3, g3 = vectors(qg3, c)
        emit(c, 2, (ds2 * q + ds3 * q3, p2 * g + p3 * g3))
        put(own_grads, c, 0, (p2 * v, ds2 * k))

    def pass_on_od3(c):
        od3_1_to_2(c, 1).wait_recv()
        far = vectors(od_b, c + heads)
        put(send_c, c, 0, [own_grads[c + heads, a] + far[a] for a in range(2)])
        at_last(od_2_to_3, c, start, every)

    def finish_2(c):
        at_first(qg2_copy, c, gone, lead)
        at_first(qg3_forward, c, gone, lead)
        at_first(sc_2_to_1, c, gone)

        def done(late):
            at_first(grads_2_to_0, late, gone, edge)
            at_first(grads_2_to_1, late, gone, opening)
            at_first(scd_2_to_3, late, gone, every)
            at_first(od_2_to_3, late, gone, every)

        each(heads + 3 * c, heads + 3 * c + 3, done)
        at_first(scd_forward, c, gone, every)
        at_first(od_2_to_3, c, gone, every)

        @pl.when(c > 0)
        def _():
            for a in range(4):
                join(a, c)

        @pl.when(c == 0)
        def _():
            join(2, 0)
            join(3, 0)

        od_1_to_2(c, 1).wait_recv()
        far = vectors(od_b, c)
        emit_late(c, [own_grads[c, a] + far[a] for a in range(2)])

    def chunk_3(c):
        at_first(scd_2_to_3, c, received, every)
        own, far = sc_stage[0, c], scd[c]
        p = jnp.exp(own[0:1] - far[0:1])
        ds = p * (own[1:2] - far[1:2]) * scaling
        p, ds = to_columns(stack_rows([p, ds]), 2)
        q, g, k, v = vectors(cols_in, c)
        emit(c, 2, (ds * q, p * g))
        at_first(qg3_copy, c, gone, every)
        at_first(sc_3_to_2, c, gone, every)
        own = (p * v, ds * k)

        @pl.when(c >= heads)
        def _():
            at_first(od_2_to_3, c, received, every)
            near = vectors(od_a, c)
            emit(c, 0, (own[0] + near[0], own[1] + near[1]))

        @pl.when(c < heads)
        def _():
            put(own_grads, c, 0, own)

    def finish_3(c):
        at_first(od_2_to_3, c, received, every)
        far = vectors(od_a, c)
        emit_late(c, [own_grads[c, a] + far[a] for a in range(2)])

    ends = (me == 0) | (me == 3)
    first_row = jnp.where(me == 1, 3 * heads, jnp.where(me == 2, 1, -3 * heads))
    first_step = jnp.where(ends, -3 * heads, 0)
    steps = jnp.where(me == 1, chunks + 2 * heads, chunks)

    def body(t):
        piece = t - first_row
        here = (piece >= 0) & (piece < 2 * heads)

        @pl.when(here & (piece % 2 == 0))
        def _():
            row_piece(rows_in, acc, rows_stage, piece // 2, 1, tokens, depth)

        @pl.when(here & (piece % 2 == 1))
        def _():
            row_piece(rows_in, acc, rows_stage, piece // 2, 0, tokens, depth)

        rest = piece - 2 * heads

        @pl.when((rest >= 0) & (rest < QUARTERS))
        def _():
            place_rows(rest)

        @pl.when(ends & ((t == heads) | (t == 2 * heads) | (t == 3 * heads)))
        def _():
            quarter = jnp.where((me == 0) & (t == 3 * heads), 0, t // heads)
            for a in range(4):
                join(a, quarter)

        @pl.when((me == 0) & (t >= 0))
        def _():
            chunk_0(t)

        @pl.when((me == 1) & (t >= 0) & (t < 3 * heads))
        def _():
            chunk_1a(t)

        @pl.when((me == 1) & (t >= FIRST_B) & (t < FIRST_B + heads))
        def _():
            chunk_1b(t - FIRST_B)

        @pl.when((me == 1) & (t == 3 * heads - 1))
        def _():
            each(0, heads, lambda c: od3_1_to_2(c, 1).start())
            each(0, heads, lambda c: od_1_to_2(c, 1).start())

        @pl.when((me == 2) & (t < 3 * heads))
        def _():
            chunk_2a(t)

        @pl.when((me == 2) & (t >= 2 * heads) & (t < 3 * heads))
        def _():
            chunk_2b(t - 2 * heads)

        @pl.when((me == 3) & (t >= 0))
        def _():
            @pl.when(t < 3 * heads)
            def _():
                chunk_3(t + heads)

            @pl.when((t >= 2 * heads) & (t < 3 * heads))
            def _():
                chunk_3(t - 2 * heads)

    each(first_step, steps, body)

    @pl.when(me == 1)
    def _():
        join(2, 0)
        join(3, 0)

        def join_early(quarter):
            join(0, quarter)
            join(1, quarter)

        each(0, QUARTERS, join_early)

        def finish(c):
            at_first(kv0_forward, c, gone, every)
            at_first(kv1_copy, c, gone, every)
            at_first(grads_1_to_0, c, gone, every)

            @pl.when(c == chunks - 2)
            def _():
                each(0, heads, done_b)

            at_first(grads_2_to_1, c, received, opening)
            far = vectors(grads_a, c)
            total = [own_grads[c, a] + far[a] for a in range(2)]

            @pl.when(c < chunks - heads)
            def _():
                emit(c, 2, total)

            @pl.when(c >= chunks - heads)
            def _():
                emit_late(c, total)

            @pl.when((c % heads == heads - 1) & (c < chunks - 1))
            def _():
                join(2, c // heads)
                join(3, c // heads)

        def done_b(c):
            at_first(grads_1_to_0, c, gone, every)
            at_first(scd_1_to_2, c, gone)
            od3_1_to_2(c, 1).wait_send()
            od_1_to_2(c, 1).wait_send()

        each(heads, chunks, finish)

    @pl.when(me == 3)
    def _():
        join(2, 0)
        join(3, 0)
        each(0, heads, finish_3)

    @pl.when(me == 2)
    def _():
        each(0, heads, pass_on_od3)
        each(0, heads, finish_2)


FIRST_B = 7


def store_kernel(*refs):
    ins, late, outs, last, leave = refs[:4], refs[4], refs[5:9], refs[9], refs[10]
    tokens, local_heads, depth = ins[0].shape
    columns = tokens // QUARTERS
    me = lax.axis_index("ctx")

    def send(a, first, count):
        part = pl.ds(first * columns, count * columns)
        return pltpu.make_async_copy(ins[a].at[part], outs[a].at[part], leave.at[a])

    def send_last(a, quarter):
        part = pl.ds(quarter * columns, columns)
        return pltpu.make_async_copy(last.at[a % 2], outs[a].at[part], leave.at[4 + a % 2])

    def store(arrays, others, first, quarter):
        whole = [send(a, 0, QUARTERS) for a in others] + [send(a, first, QUARTERS - 1) for a in arrays]
        for copy in whole:
            copy.start()
        for i, a in enumerate(arrays):
            last[i] = late[i].reshape(columns, local_heads, depth).astype(BF16)
            send_last(a, quarter).start()
        for copy in whole:
            copy.wait()
        for a in arrays:
            send_last(a, quarter).wait()

    @pl.when(me < 2)
    def _():
        store((2, 3), (0, 1), 0, QUARTERS - 1)

    @pl.when(me >= 2)
    def _():
        store((0, 1), (2, 3), 1, 0)


def fused(queries, key_vecs, value_vecs, grad_out):
    shape = queries.shape
    tokens, local_heads, depth = shape[2:]
    heads = local_heads // 2
    columns = tokens // QUARTERS
    chunks = heads * QUARTERS
    flat = [
        pltpu.with_memory_space_constraint(x.reshape(tokens, local_heads, depth), pltpu.HBM)
        for x in (queries, key_vecs, value_vecs, grad_out)
    ]
    hbm = pl.BlockSpec(memory_space=pltpu.HBM)
    vmem = pl.BlockSpec(memory_space=pltpu.VMEM)
    two = pltpu.VMEM((chunks, 2, columns, depth), BF16)
    few = pltpu.VMEM((heads, 2, columns, depth), BF16)
    four = pltpu.VMEM((chunks, 4, columns, depth), BF16)
    row_buf = pltpu.VMEM((heads, 4, tokens, depth), BF16)
    flat_rows = pltpu.VMEM((chunks, 8, columns), F32)
    dma = pltpu.SemaphoreType.DMA
    parts = pl.pallas_call(
        kernel,
        out_shape=[pltpu.VMEM((tokens, local_heads, depth), BF16)] * 4
        + [pltpu.VMEM((2, columns * local_heads, depth), F32)],
        in_specs=[hbm] * 4,
        out_specs=[vmem] * 5,
        scratch_shapes=[
            pltpu.VMEM((4, tokens, local_heads, depth), BF16),
            pltpu.VMEM((4, columns * local_heads, depth), F32),
            row_buf, four, row_buf,
            pltpu.VMEM((4, QUARTERS, columns * local_heads, depth), F32),
            pltpu.VMEM((2, tokens // 2, depth), F32),
            pltpu.VMEM((chunks, 2, columns, depth), F32),
            two, two, few, two, flat_rows, two, two, two, two, flat_rows,
            pltpu.VMEM((2, chunks, 8, columns), F32), flat_rows,
            two, two, two,
            dma((4, QUARTERS)), dma((7, chunks)), dma((10, chunks)),
        ],
        compiler_params=pltpu.CompilerParams(
            collective_id=0, has_side_effects=True, vmem_limit_bytes=44 * 1024 * 1024
        ),
    )(*flat)
    results = pl.pallas_call(
        store_kernel,
        out_shape=[jax.ShapeDtypeStruct((tokens, local_heads, depth), BF16)] * 4,
        in_specs=[vmem] * 5,
        out_specs=[pl.BlockSpec(memory_space=pl.ANY)] * 4,
        scratch_shapes=[pltpu.VMEM((2, columns, local_heads, depth), BF16), dma((6,))],
        compiler_params=pltpu.CompilerParams(vmem_limit_bytes=2 * 1024 * 1024),
    )(*parts)
    return tuple(x.reshape(shape) for x in results)


def causal(length):
    positions = jnp.arange(length)
    return positions[None, :] <= positions[:, None]


def attend(query_in, key_in, value_in, grad_in, layout, allowed):
    scaling = 1.0 / math.sqrt(query_in.shape[-1])
    key_form = layout.replace("q", "k")
    scores = (
        jnp.einsum(
            layout + "," + key_form + "->bxhqk",
            query_in,
            key_in,
            preferred_element_type=jnp.float32,
        )
        * scaling
    )
    scores = jnp.where(allowed, scores, -1e30)
    highest = jnp.max(scores, axis=-1, keepdims=True)
    weight_sum = jnp.sum(jnp.exp(scores - highest), axis=-1, keepdims=True)
    log_total = highest + jnp.log(weight_sum)
    weights = jnp.where(allowed, jnp.exp(scores - log_total), 0.0)
    rounded = weights.astype(jnp.bfloat16)
    output = jnp.einsum(
        "bxhqk," + key_form + "->" + layout, rounded, value_in, preferred_element_type=jnp.float32
    ).astype(jnp.bfloat16)
    row_dots = jnp.einsum(
        layout + "," + layout + "->bxhq", grad_in, output, preferred_element_type=jnp.float32
    )
    dprobs = jnp.einsum(
        layout + "," + key_form + "->bxhqk", grad_in, value_in, preferred_element_type=jnp.float32
    )
    dscores = (weights * (dprobs - row_dots[..., None]) * scaling).astype(jnp.bfloat16)
    grad_query = jnp.einsum(
        "bxhqk," + key_form + "->" + layout, dscores, key_in, preferred_element_type=jnp.float32
    ).astype(jnp.bfloat16)
    grad_key = jnp.einsum(
        "bxhqk," + layout + "->" + key_form, dscores, query_in, preferred_element_type=jnp.float32
    )
    grad_value = jnp.einsum(
        "bxhqk," + layout + "->" + key_form, rounded, grad_in, preferred_element_type=jnp.float32
    )
    return (output, grad_query, grad_key, grad_value)


def merge_heads(first_part, second_part):
    stacked = jnp.stack((first_part, second_part), axis=4)
    shape = first_part.shape
    return stacked.reshape(shape[:3] + (2 * shape[3], shape[4]))


def per_device(queries, key_vecs, value_vecs, grad_out):
    arrays = (queries, key_vecs, value_vecs, grad_out)
    row_parts = tuple((array[:, :, :, 0::2] for array in arrays))
    col_parts = tuple((array[:, :, :, 1::2] for array in arrays))
    row_local = attend(
        row_parts[0], row_parts[1], row_parts[2], row_parts[3], "bxqhd", causal(queries.shape[2])
    )
    row_results = (
        row_local[0],
        row_local[1],
        row_local[2].astype(jnp.bfloat16),
        row_local[3].astype(jnp.bfloat16),
    )
    local_rows = col_parts[0].shape[1]
    gathered = (
        lax.all_gather(col_parts[1], "ctx", axis=1, tiled=True),
        lax.all_gather(col_parts[2], "ctx", axis=1, tiled=True),
    )
    query_rows = lax.axis_index("ctx") * local_rows + jnp.arange(local_rows)
    key_rows = jnp.arange(gathered[0].shape[1])
    allowed = key_rows[None, :] <= query_rows[:, None]
    col_local = attend(col_parts[0], gathered[0], gathered[1], col_parts[3], "bqxhd", allowed)
    summed = (
        lax.psum_scatter(col_local[2], "ctx", scatter_dimension=1, tiled=True),
        lax.psum_scatter(col_local[3], "ctx", scatter_dimension=1, tiled=True),
    )
    col_results = (
        col_local[0],
        col_local[1],
        summed[0].astype(jnp.bfloat16),
        summed[1].astype(jnp.bfloat16),
    )
    return (
        merge_heads(row_results[0], col_results[0]),
        merge_heads(row_results[1], col_results[1]),
        merge_heads(row_results[2], col_results[2]),
        merge_heads(row_results[3], col_results[3]),
    )


def solution(mesh):
    body = fused if mesh.shape["ctx"] == 4 else per_device
    placed = (
        P(("groups", "dp"), "ctx", None, "head", None),
        P(("groups", "dp"), "ctx", None, "head", None),
        P(("groups", "dp"), "ctx", None, "head", None),
        P(("groups", "dp"), "ctx", None, "head", None),
    )
    return jax.shard_map(
        body,
        mesh=mesh,
        in_specs=placed,
        out_specs=(
            P(("groups", "dp"), "ctx", None, "head", None),
            P(("groups", "dp"), "ctx", None, "head", None),
            P(("groups", "dp"), "ctx", None, "head", None),
            P(("groups", "dp"), "ctx", None, "head", None),
        ),
        check_vma=False,
    )
```

```python
import functools
import math

import jax
import jax.numpy as jnp
from jax import lax
from jax.experimental import pallas as pl
from jax.experimental.pallas import tpu as pltpu
from jax.sharding import PartitionSpec as P

MESH = pl.DeviceIdType.MESH
F32 = jnp.float32
BF16 = jnp.bfloat16
NT = (((1,), (1,)), ((), ()))
NN = (((1,), (0,)), ((), ()))
TN = (((0,), (0,)), ((), ()))


def mm(a, b, dims):
    return lax.dot_general(a, b, dims, preferred_element_type=F32)


def row_piece(buf, acc, stage, i, b, tokens, depth):
    scaling = 1.0 / math.sqrt(depth)
    block = tokens // 2
    rows = pl.ds(b * block, block)
    span = (b + 1) * block
    q = buf[i, Q, rows]
    g = buf[i, G, rows]
    k = buf[i, K, pl.ds(0, span)]
    v = buf[i, V, pl.ds(0, span)]
    s = mm(q, k, NT) * scaling
    qpos = lax.broadcasted_iota(jnp.int32, (block, span), 0) + b * block
    kpos = lax.broadcasted_iota(jnp.int32, (block, span), 1)
    s = jnp.where(kpos <= qpos, s, -1e30)
    top = jnp.max(s, axis=-1, keepdims=True)
    e = jnp.exp(s - top)
    p = e * (1.0 / jnp.sum(e, axis=-1, keepdims=True))
    pb = p.astype(BF16)
    o = mm(pb, v, NN).astype(BF16)
    dots = jnp.sum(g.astype(F32) * o.astype(F32), axis=-1, keepdims=True)
    dp = mm(g, v, NT)
    ds = (p * (dp - dots) * scaling).astype(BF16)
    stage[i, 0, rows] = o
    stage[i, 1, rows] = mm(ds, k, NN).astype(BF16)
    dk = mm(ds, q, TN)
    dv = mm(pb, g, TN)
    if b == 1:
        acc[0] = dk[:block]
        acc[1] = dv[:block]
        stage[i, 2, rows] = dk[block:].astype(BF16)
        stage[i, 3, rows] = dv[block:].astype(BF16)
    else:
        stage[i, 2, rows] = (acc[0] + dk).astype(BF16)
        stage[i, 3, rows] = (acc[1] + dv).astype(BF16)


def dot(a, b):
    return jnp.sum(a * b, axis=-1, keepdims=True)


def add_up(terms):
    return functools.reduce(jnp.add, terms)


def attend_to(q, g, keys, scaling, rest=None):
    s = [dot(q, k) * scaling for k, _ in keys]
    dp = [dot(g, v) for _, v in keys]
    if rest is not None:
        s, dp = s + [rest[0]], dp + [rest[1]]
    top = functools.reduce(jnp.maximum, s)
    e = [jnp.exp(x - top) for x in s]
    total = add_up(e)
    inverse = 1.0 / total
    p = [x * inverse for x in e]
    dots = add_up([x * y for x, y in zip(p, dp)])
    ds = [x * (y - dots) * scaling for x, y in zip(p, dp)]
    o = add_up([x * kv[1] for x, kv in zip(p, keys)])
    dq = add_up([x * kv[0] for x, kv in zip(ds, keys)])
    return o, dq, p, ds, top + jnp.log(total), dots


def to_rows(columns):
    tokens = columns[0].shape[0]
    lane = lax.broadcasted_iota(jnp.int32, (tokens, 128), 1)
    wide = jnp.broadcast_to(columns[0], (tokens, 128))
    for i, x in enumerate(columns[1:], 1):
        wide = jnp.where(lane == i, x, wide)
    return jnp.transpose(wide)[:8]


def stack_rows(rows):
    index = lax.broadcasted_iota(jnp.int32, (8, rows[0].shape[1]), 0)
    out = jnp.broadcast_to(rows[0], index.shape)
    for i, x in enumerate(rows[1:], 1):
        out = jnp.where(index == i, x, out)
    return out


def to_columns(rows, count):
    turned = jnp.transpose(jnp.concatenate([rows] * 16, axis=0))
    return [turned[:, i : i + 1] for i in range(count)]


Q, G, K, V = 0, 1, 2, 3
QUARTERS = 4
KV0, KV1, QG2, QG3, SC, GA, GB, OD_A, OD_B, SCD = range(10)


def start(copy):
    copy.start()


def received(copy):
    copy.wait_recv()


def gone(copy):
    copy.wait_send()


def each(first, last, body):
    def step(i, _):
        body(i)
        return 0

    lax.fori_loop(first, last, step, 0)


def kernel(
    q_ref, k_ref, v_ref, g_ref, o_out, dq_out, dk_out, dv_out, late,
    fetched, wide, rows_in, cols_in, rows_stage, joined, acc, own_grads,
    kv0, kv1, qg2, qg3, sc, grads_a, grads_b, od_a, od_b, scd,
    sc_stage, scd_stage, send_a, send_b, send_c,
    load, sent, got,
):
    tokens, local_heads, depth = q_ref.shape
    heads = local_heads // 2
    columns = tokens // QUARTERS
    chunks = heads * QUARTERS
    scaling = 1.0 / math.sqrt(depth)
    me = lax.axis_index("ctx")
    core = lax.axis_index("dp")
    refs = (q_ref, g_ref, k_ref, v_ref)
    outs = (o_out, dq_out, dk_out, dv_out)
    shift = jnp.where(me < 2, 1, 0)
    late_quarter = jnp.where(me < 2, QUARTERS - 1, 0)
    late_first = jnp.where(me < 2, 2, 0)

    barrier = pltpu.get_barrier_semaphore()

    def greet(target):
        pl.semaphore_signal(barrier, inc=1, device_id={"ctx": target}, device_id_type=MESH)

    @pl.when(me == 1)
    def _():
        greet(0)
        greet(2)

    @pl.when(me == 2)
    def _():
        greet(1)
        greet(3)

    def turn(step):
        return lax.rem(step + shift, QUARTERS)

    def fetch(at, quarter):
        part = pl.ds(quarter * columns, columns)
        return pltpu.make_async_copy(refs[at].at[part], fetched.at[at, part], load.at[at, quarter])

    def fetch_first(arrays):
        for at in arrays:
            fetch(at, turn(0)).start()

    def fetch_rest(arrays, others):
        for at in others:
            fetch(at, turn(0)).start()

        def later(step):
            for at in arrays + others:
                fetch(at, turn(step)).start()

        each(1, QUARTERS, later)

    @pl.when(me < 2)
    def _():
        fetch_first((K, V))

    @pl.when(me >= 2)
    def _():
        fetch_first((Q, G))

    def remote(src, dst, send, recv, c, slot, target):
        return pltpu.make_async_remote_copy(
            src_ref=src, dst_ref=dst, send_sem=sent.at[send, c], recv_sem=got.at[recv, slot],
            device_id={"ctx": target}, device_id_type=MESH,
        )

    def widen(at, quarter):
        fetch(at, quarter).wait()
        x = fetched[at, pl.ds(quarter * columns, columns)].astype(F32)
        wide[at] = x.reshape(columns * local_heads, depth)

    def take_row(at, quarter, i):
        x = wide[at, pl.ds(2 * i, columns, stride=local_heads)].astype(BF16)
        rows_in[i, at, pl.ds(quarter * columns, columns)] = x

    def take_column(at, quarter, i):
        x = wide[at, pl.ds(2 * i + 1, columns, stride=local_heads)].astype(BF16)
        cols_in[quarter * heads + i, at] = x

    def split(at, quarter):
        widen(at, quarter)
        for i in range(heads):
            take_row(at, quarter, i)
            take_column(at, quarter, i)

    def split_first(arrays, quarter, send, alone, both):
        for at in arrays:
            widen(at, quarter)
        pl.semaphore_wait(barrier, 1)
        for i in range(heads):
            for at in arrays:
                take_column(at, quarter, i)
            if i < alone:
                send(quarter * heads + i, 1).start()
            if i == heads - 1 and alone == 2 and both:
                send(quarter * heads + 2, 2).start()
        for i in range(heads):
            for at in arrays:
                take_row(at, quarter, i)

    def place_rows(quarter):
        part = pl.ds(quarter * columns, columns)
        for a in range(4):
            for h in range(heads):
                x = rows_stage[h, a, part].astype(F32)
                joined[a, quarter, pl.ds(2 * h, columns, stride=local_heads)] = x

        @pl.when(quarter == late_quarter)
        def _():
            for a in range(2):
                for h in range(heads):
                    x = rows_stage[h, late_first + a, part].astype(F32)
                    late[a, pl.ds(2 * h, columns, stride=local_heads)] = x

    def emit_late(c, values):
        for a, x in enumerate(values):
            late[a, pl.ds(2 * (c % heads) + 1, columns, stride=local_heads)] = x

    def emit(c, first, values):
        for a, x in enumerate(values, first):
            spots = pl.ds(2 * (c % heads) + 1, columns, stride=local_heads)
            joined[a, c // heads, spots] = x.astype(F32)

    def join(a, quarter):
        part = pl.ds(quarter * columns, columns)
        outs[a][part] = joined[a, quarter].reshape(columns, local_heads, depth).astype(BF16)

    def vectors(buf, c):
        return [buf[c, a].astype(F32) for a in range(buf.shape[1])]

    def put(ref, c, first, values):
        for a, x in enumerate(values):
            ref[c, first + a] = x.astype(ref.dtype)

    def flow(src, dst, send, recv, target, shift=0):
        def copy(c, n):
            return remote(
                src(pl.ds(c, n)), dst.at[pl.ds(c + shift, n)], send, recv, c, c + shift, target
            )

        return copy

    def whole(buf):
        return lambda part: buf.at[part]

    def halves(first):
        return lambda part: cols_in.at[part, pl.ds(first, 2)]

    kv0_copy = flow(halves(K), kv0, 0, KV0, 1)
    kv0_forward = flow(whole(kv0), kv0, 0, KV0, 2)
    kv1_copy = flow(halves(K), kv1, 1, KV1, 2)
    grads_1_to_0 = flow(whole(send_a), grads_b, 2, GB, 0)
    od_1_to_2 = flow(whole(send_b), od_b, 3, OD_B, 2)
    od3_1_to_2 = flow(whole(send_c), od_b, 4, OD_B, 2, heads)
    scd_1_to_2 = flow(whole(scd_stage), scd, 5, SCD, 2)
    scd_forward = flow(whole(scd), scd, 6, SCD, 3)
    qg2_copy = flow(halves(Q), qg2, 0, QG2, 1)
    qg3_forward = flow(whole(qg3), qg3, 1, QG3, 1)
    sc_2_to_1 = flow(lambda part: sc_stage.at[1, part], sc, 2, SC, 1)
    grads_2_to_0 = flow(whole(send_a), grads_a, 3, GA, 0)
    grads_2_to_1 = flow(whole(send_b), grads_a, 4, GA, 1)
    od_2_to_3 = flow(whole(send_c), od_a, 5, OD_A, 3)
    scd_2_to_3 = flow(whole(scd_stage), scd, 6, SCD, 3)
    qg3_copy = flow(halves(Q), qg3, 0, QG3, 2)
    sc_3_to_2 = flow(lambda part: sc_stage.at[0, part], sc, 1, SC, 2)

    def opening(c):
        return (c >= heads) & (c < heads + 2)

    def lead(c):
        return (c < 2) | opening(c)

    def every(c):
        return c >= 0

    def edge(c):
        return opening(c) | (c >= chunks - 2)

    def at_first(copy, c, act, alone=None):
        if alone is None:
            pl.when(c % 2 == 0)(lambda: act(copy(c, 2)))
        else:
            pl.when(alone(c))(lambda: act(copy(c, 1)))
            pl.when(jnp.logical_not(alone(c)) & (c % 2 == 0))(lambda: act(copy(c, 2)))

    def at_last(copy, c, act, alone=None):
        if alone is None:
            pl.when(c % 2 == 1)(lambda: act(copy(c - 1, 2)))
        else:
            pl.when(alone(c))(lambda: act(copy(c, 1)))
            pl.when(jnp.logical_not(alone(c)) & (c % 2 == 1))(lambda: act(copy(c - 1, 2)))

    @pl.when(me == 0)
    def _():
        split_first((K, V), 1, kv0_copy, heads, True)
        fetch_rest((K, V), (Q, G))

        def go(step):
            quarter = turn(step)

            @pl.when(step > 0)
            def _():
                split(K, quarter)
                split(V, quarter)
                each(0, heads, lambda i: kv0_copy(quarter * heads + i, 1).start())

            split(Q, quarter)
            split(G, quarter)

        each(0, QUARTERS, go)

    @pl.when(me == 1)
    def _():
        split_first((K, V), 1, kv1_copy, 2, False)
        fetch_rest((K, V), (Q, G))

    @pl.when(me == 2)
    def _():
        split_first((Q, G), 0, qg2_copy, 2, True)
        fetch_rest((Q, G), (K, V))
        split(K, 0)
        split(V, 0)

        def pass_on(c):
            at_first(qg3_copy, c, received, every)
            at_last(qg3_forward, c, start, lead)
            q, g, k, v = vectors(cols_in, c)
            q3, g3 = vectors(qg3, c)
            own = to_rows([dot(q, k) * scaling, dot(g, v), dot(q3, k) * scaling, dot(g3, v)])
            sc_stage[0, c] = own

            @pl.when(c < QUARTERS - 1)
            def _():
                for at in range(4):
                    split(at, c + 1)

        each(0, heads, pass_on)

        def merge(c):
            at_first(sc_3_to_2, c, received, every)
            own, far = sc_stage[0, c], sc[c]
            s32, dp32, s33, dp33 = own[2:3], own[3:4], far[0:1], far[1:2]
            top = jnp.maximum(s32, s33)
            e32, e33 = jnp.exp(s32 - top), jnp.exp(s33 - top)
            total = e32 + e33
            mean = (e32 * dp32 + e33 * dp33) / total
            sc_stage[1, c] = stack_rows([own[0:1], own[1:2], top + jnp.log(total), mean])
            at_last(sc_2_to_1, c, start)

        each(0, heads, merge)

    @pl.when(me == 3)
    def _():
        split_first((Q, G), 0, qg3_copy, heads, True)
        fetch_rest((Q, G), (K, V))

        def go(quarter):
            @pl.when(quarter > 0)
            def _():
                split(Q, quarter)
                split(G, quarter)

            split(K, quarter)
            split(V, quarter)

            def scores(i):
                c = quarter * heads + i

                @pl.when(quarter > 0)
                def _():
                    at_first(qg3_copy, c, start, every)

                q, g, k, v = vectors(cols_in, c)
                sc_stage[0, c] = to_rows([dot(q, k) * scaling, dot(g, v)])
                at_last(sc_3_to_2, c, start, every)

            each(0, heads, scores)

        each(0, QUARTERS, go)

    def chunk_0(t):
        c = jnp.where(t < 2 * heads, t + heads, jnp.where(t < 3 * heads, t - 2 * heads, t))
        q, g, k, v = vectors(cols_in, c)
        o, dq, p, ds, _, _ = attend_to(q, g, [(k, v)], scaling)
        emit(c, 0, (o, dq))
        at_first(kv0_copy, c, gone, every)

        @pl.when(t == chunks - 1)
        def _():
            join(0, 3)
            join(1, 3)

        at_first(grads_1_to_0, c, received, every)
        near = vectors(grads_b, c)
        total = (ds[0] * q + near[0], p[0] * g + near[1])

        @pl.when(c < heads)
        def _():
            emit(c, 2, total)

        @pl.when(c >= heads)
        def _():
            at_first(grads_2_to_0, c, received, edge)
            far = vectors(grads_a, c)
            whole = (total[0] + far[0], total[1] + far[1])

            @pl.when(c < chunks - heads)
            def _():
                emit(c, 2, whole)

            @pl.when(c >= chunks - heads)
            def _():
                emit_late(c, whole)

    def chunk_1a(t):
        c = t + heads
        at_first(kv0_copy, c, received, every)
        at_first(kv0_forward, c, start, every)

        @pl.when((t % 2 == 1) & (t <= 5))
        def _():
            split(K, (t // 2 + 2) % QUARTERS)
            split(V, (t // 2 + 2) % QUARTERS)

        @pl.when(c + 2 < chunks)
        def _():
            kv1_copy(c + 2, 1).start()

        @pl.when((t % 2 == 0) & (t <= 6))
        def _():
            split(Q, (t // 2 + 1) % QUARTERS)
            split(G, (t // 2 + 1) % QUARTERS)

        q, g, k, v = vectors(cols_in, c)
        k0, v0 = vectors(kv0, c)
        o, dq, p, ds, _, _ = attend_to(q, g, [(k0, v0), (k, v)], scaling)
        put(send_a, c, 0, (ds[0] * q, p[0] * g))
        at_last(grads_1_to_0, c, start, every)
        emit(c, 0, (o, dq))
        put(own_grads, c, 0, (ds[1] * q, p[1] * g))

    def chunk_1b(c):
        at_first(kv0_copy, c, received, every)
        at_first(qg2_copy, c, received, lead)
        at_first(qg3_forward, c, received, lead)
        at_first(sc_2_to_1, c, received)
        q, g, k, v = vectors(cols_in, c)
        k0, v0 = vectors(kv0, c)
        keys = [(k0, v0), (k, v)]
        rest = to_columns(sc[c], 4)
        q2, g2 = vectors(qg2, c)
        o2, dq2, p2, ds2, lse2, dots2 = attend_to(q2, g2, keys, scaling, rest[:2])
        q3, g3 = vectors(qg3, c)
        o3, dq3, p3, ds3, lse3, dots3 = attend_to(q3, g3, keys, scaling, rest[2:])
        scd_stage[c] = to_rows([lse3, dots3, lse2, dots2])
        at_last(scd_1_to_2, c, start)
        put(send_b, c, 0, (o2, dq2))
        put(send_c, c, 0, (o3, dq3))

        o, dq, p, ds, _, _ = attend_to(q, g, keys, scaling)
        emit(c, 0, (o, dq))
        dk = [ds[j] * q + ds2[j] * q2 + ds3[j] * q3 for j in range(2)]
        dv = [p[j] * g + p2[j] * g2 + p3[j] * g3 for j in range(2)]
        put(send_a, c, 0, (dk[0], dv[0]))
        at_last(grads_1_to_0, c, start, every)
        emit(c, 2, (dk[1], dv[1]))

    def chunk_2a(t):
        c = t + heads
        at_first(kv1_copy, c, received, every)
        at_first(kv0_forward, c, received, every)
        at_first(qg3_copy, c, received, every)
        at_first(sc_3_to_2, c, received, every)
        q, g, k, v = vectors(cols_in, c)
        q3, g3 = vectors(qg3, c)
        k0, v0 = vectors(kv0, c)
        k1, v1 = vectors(kv1, c)
        keys = [(k0, v0), (k1, v1), (k, v)]
        rest = to_columns(sc[c], 2)
        o, dq, p, ds, _, _ = attend_to(q, g, keys, scaling)
        o3, dq3, p3, ds3, lse3, dots3 = attend_to(q3, g3, keys, scaling, rest)
        dk = [ds[j] * q + ds3[j] * q3 for j in range(3)]
        dv = [p[j] * g + p3[j] * g3 for j in range(3)]
        put(send_a, c, 0, (dk[0], dv[0]))
        at_last(grads_2_to_0, c, start, edge)
        put(send_b, c, 0, (dk[1], dv[1]))

        @pl.when(core > 0)
        def _():
            at_last(grads_2_to_1, c, start, edge)

        @pl.when((core == 0) & (t < 2))
        def _():
            grads_2_to_1(c, 1).start()

        @pl.when((core == 0) & (t >= heads))
        def _():
            at_last(grads_2_to_1, c - 2, start)

        @pl.when((core == 0) & (t == 3 * heads - 1))
        def _():
            each(chunks - 2, chunks, lambda late: grads_2_to_1(late, 1).start())

        scd_stage[c] = to_rows([lse3, dots3])
        at_last(scd_2_to_3, c, start, every)
        put(send_c, c, 0, (o3, dq3))
        at_last(od_2_to_3, c, start, every)
        emit(c, 0, (o, dq, dk[2], dv[2]))

    def chunk_2b(c):
        at_first(scd_1_to_2, c, received)
        at_first(scd_forward, c, start, every)
        own, far = sc_stage[0, c], scd[c]
        p3 = jnp.exp(own[2:3] - far[0:1])
        ds3 = p3 * (own[3:4] - far[1:2]) * scaling
        p2 = jnp.exp(own[0:1] - far[2:3])
        ds2 = p2 * (own[1:2] - far[3:4]) * scaling
        p3, ds3, p2, ds2 = to_columns(stack_rows([p3, ds3, p2, ds2]), 4)
        q, g, k, v = vectors(cols_in, c)
        put(own_grads, c + heads, 0, (p3 * v, ds3 * k))
        q3, g3 = vectors(qg3, c)
        emit(c, 2, (ds2 * q + ds3 * q3, p2 * g + p3 * g3))
        put(own_grads, c, 0, (p2 * v, ds2 * k))

    def pass_on_od3(c):
        od3_1_to_2(c, 1).wait_recv()
        far = vectors(od_b, c + heads)
        put(send_c, c, 0, [own_grads[c + heads, a] + far[a] for a in range(2)])
        at_last(od_2_to_3, c, start, every)

    def finish_2(c):
        at_first(qg2_copy, c, gone, lead)
        at_first(qg3_forward, c, gone, lead)
        at_first(sc_2_to_1, c, gone)

        def done(late):
            at_first(grads_2_to_0, late, gone, edge)
            at_first(grads_2_to_1, late, gone, edge)
            at_first(scd_2_to_3, late, gone, every)
            at_first(od_2_to_3, late, gone, every)

        each(heads + 3 * c, heads + 3 * c + 3, done)
        at_first(scd_forward, c, gone, every)
        at_first(od_2_to_3, c, gone, every)

        @pl.when(c > 0)
        def _():
            for a in range(4):
                join(a, c)

        @pl.when(c == 0)
        def _():
            join(2, 0)
            join(3, 0)

        od_1_to_2(c, 1).wait_recv()
        far = vectors(od_b, c)
        emit_late(c, [own_grads[c, a] + far[a] for a in range(2)])

    def chunk_3(c):
        at_first(scd_2_to_3, c, received, every)
        own, far = sc_stage[0, c], scd[c]
        p = jnp.exp(own[0:1] - far[0:1])
        ds = p * (own[1:2] - far[1:2]) * scaling
        p, ds = to_columns(stack_rows([p, ds]), 2)
        q, g, k, v = vectors(cols_in, c)
        emit(c, 2, (ds * q, p * g))
        at_first(qg3_copy, c, gone, every)
        at_first(sc_3_to_2, c, gone, every)
        own = (p * v, ds * k)

        @pl.when(c >= heads)
        def _():
            at_first(od_2_to_3, c, received, every)
            near = vectors(od_a, c)
            emit(c, 0, (own[0] + near[0], own[1] + near[1]))

        @pl.when(c < heads)
        def _():
            put(own_grads, c, 0, own)

    def finish_3(c):
        at_first(od_2_to_3, c, received, every)
        far = vectors(od_a, c)
        emit_late(c, [own_grads[c, a] + far[a] for a in range(2)])

    ends = (me == 0) | (me == 3)
    first_row = jnp.where(me == 1, 3 * heads, jnp.where(me == 2, 1, -3 * heads))
    first_step = jnp.where(ends, -3 * heads, 0)
    steps = jnp.where(me == 1, chunks + 2 * heads, chunks)

    def body(t):
        piece = t - first_row
        here = (piece >= 0) & (piece < 2 * heads)

        @pl.when(here & (piece % 2 == 0))
        def _():
            row_piece(rows_in, acc, rows_stage, piece // 2, 1, tokens, depth)

        @pl.when(here & (piece % 2 == 1))
        def _():
            row_piece(rows_in, acc, rows_stage, piece // 2, 0, tokens, depth)

        rest = piece - 2 * heads

        @pl.when((rest >= 0) & (rest < QUARTERS))
        def _():
            place_rows(rest)

        @pl.when(ends & ((t == heads) | (t == 2 * heads) | (t == 3 * heads)))
        def _():
            quarter = jnp.where((me == 0) & (t == 3 * heads), 0, t // heads)
            for a in range(4):
                join(a, quarter)

        @pl.when((me == 0) & (t >= 0))
        def _():
            chunk_0(t)

        @pl.when((me == 1) & (t >= 0) & (t < 3 * heads))
        def _():
            chunk_1a(t)

        @pl.when((me == 1) & (t >= FIRST_B) & (t < FIRST_B + heads))
        def _():
            chunk_1b(t - FIRST_B)

        @pl.when((me == 1) & (t == 3 * heads - 1))
        def _():
            each(0, heads, lambda c: od3_1_to_2(c, 1).start())
            each(0, heads, lambda c: od_1_to_2(c, 1).start())

        @pl.when((me == 2) & (t < 3 * heads))
        def _():
            chunk_2a(t)

        @pl.when((me == 2) & (t >= 2 * heads) & (t < 3 * heads))
        def _():
            chunk_2b(t - 2 * heads)

        @pl.when((me == 3) & (t >= 0))
        def _():
            @pl.when(t < 3 * heads)
            def _():
                chunk_3(t + heads)

            @pl.when((t >= 2 * heads) & (t < 3 * heads))
            def _():
                chunk_3(t - 2 * heads)

    each(first_step, steps, body)

    @pl.when(me == 1)
    def _():
        join(2, 0)
        join(3, 0)

        def join_early(quarter):
            join(0, quarter)
            join(1, quarter)

        each(0, QUARTERS, join_early)

        def finish(c):
            at_first(kv0_forward, c, gone, every)
            at_first(kv1_copy, c, gone, every)
            at_first(grads_1_to_0, c, gone, every)

            @pl.when(c == chunks - 2)
            def _():
                each(0, heads, done_b)

            at_first(grads_2_to_1, c, received, edge)
            far = vectors(grads_a, c)
            total = [own_grads[c, a] + far[a] for a in range(2)]

            @pl.when(c < chunks - heads)
            def _():
                emit(c, 2, total)

            @pl.when(c >= chunks - heads)
            def _():
                emit_late(c, total)

            @pl.when((c % heads == heads - 1) & (c < chunks - 1))
            def _():
                join(2, c // heads)
                join(3, c // heads)

        def done_b(c):
            at_first(grads_1_to_0, c, gone, every)
            at_first(scd_1_to_2, c, gone)
            od3_1_to_2(c, 1).wait_send()
            od_1_to_2(c, 1).wait_send()

        each(heads, chunks, finish)

    @pl.when(me == 3)
    def _():
        join(2, 0)
        join(3, 0)
        each(0, heads, finish_3)

    @pl.when(me == 2)
    def _():
        each(0, heads, pass_on_od3)
        each(0, heads, finish_2)


FIRST_B = 7


def store_kernel(*refs):
    ins, late, outs, last, leave = refs[:4], refs[4], refs[5:9], refs[9], refs[10]
    tokens, local_heads, depth = ins[0].shape
    columns = tokens // QUARTERS
    me = lax.axis_index("ctx")

    def send(a, first, count):
        part = pl.ds(first * columns, count * columns)
        return pltpu.make_async_copy(ins[a].at[part], outs[a].at[part], leave.at[a])

    def send_last(a, quarter):
        part = pl.ds(quarter * columns, columns)
        return pltpu.make_async_copy(last.at[a % 2], outs[a].at[part], leave.at[4 + a % 2])

    def store(arrays, others, first, quarter):
        whole = [send(a, 0, QUARTERS) for a in others] + [send(a, first, QUARTERS - 1) for a in arrays]
        for copy in whole:
            copy.start()
        for i, a in enumerate(arrays):
            last[i] = late[i].reshape(columns, local_heads, depth).astype(BF16)
            send_last(a, quarter).start()
        for copy in whole:
            copy.wait()
        for a in arrays:
            send_last(a, quarter).wait()

    @pl.when(me < 2)
    def _():
        store((2, 3), (0, 1), 0, QUARTERS - 1)

    @pl.when(me >= 2)
    def _():
        store((0, 1), (2, 3), 1, 0)


def fused(queries, key_vecs, value_vecs, grad_out):
    shape = queries.shape
    tokens, local_heads, depth = shape[2:]
    heads = local_heads // 2
    columns = tokens // QUARTERS
    chunks = heads * QUARTERS
    flat = [
        pltpu.with_memory_space_constraint(x.reshape(tokens, local_heads, depth), pltpu.HBM)
        for x in (queries, key_vecs, value_vecs, grad_out)
    ]
    hbm = pl.BlockSpec(memory_space=pltpu.HBM)
    vmem = pl.BlockSpec(memory_space=pltpu.VMEM)
    two = pltpu.VMEM((chunks, 2, columns, depth), BF16)
    few = pltpu.VMEM((heads, 2, columns, depth), BF16)
    four = pltpu.VMEM((chunks, 4, columns, depth), BF16)
    row_buf = pltpu.VMEM((heads, 4, tokens, depth), BF16)
    flat_rows = pltpu.VMEM((chunks, 8, columns), F32)
    dma = pltpu.SemaphoreType.DMA
    parts = pl.pallas_call(
        kernel,
        out_shape=[pltpu.VMEM((tokens, local_heads, depth), BF16)] * 4
        + [pltpu.VMEM((2, columns * local_heads, depth), F32)],
        in_specs=[hbm] * 4,
        out_specs=[vmem] * 5,
        scratch_shapes=[
            pltpu.VMEM((4, tokens, local_heads, depth), BF16),
            pltpu.VMEM((4, columns * local_heads, depth), F32),
            row_buf, four, row_buf,
            pltpu.VMEM((4, QUARTERS, columns * local_heads, depth), F32),
            pltpu.VMEM((2, tokens // 2, depth), F32),
            pltpu.VMEM((chunks, 2, columns, depth), F32),
            two, two, few, two, flat_rows, two, two, two, two, flat_rows,
            pltpu.VMEM((2, chunks, 8, columns), F32), flat_rows,
            two, two, two,
            dma((4, QUARTERS)), dma((7, chunks)), dma((10, chunks)),
        ],
        compiler_params=pltpu.CompilerParams(
            collective_id=0, has_side_effects=True, vmem_limit_bytes=44 * 1024 * 1024
        ),
    )(*flat)
    results = pl.pallas_call(
        store_kernel,
        out_shape=[jax.ShapeDtypeStruct((tokens, local_heads, depth), BF16)] * 4,
        in_specs=[vmem] * 5,
        out_specs=[pl.BlockSpec(memory_space=pl.ANY)] * 4,
        scratch_shapes=[pltpu.VMEM((2, columns, local_heads, depth), BF16), dma((6,))],
        compiler_params=pltpu.CompilerParams(vmem_limit_bytes=2 * 1024 * 1024),
    )(*parts)
    return tuple(x.reshape(shape) for x in results)


def causal(length):
    positions = jnp.arange(length)
    return positions[None, :] <= positions[:, None]


def attend(query_in, key_in, value_in, grad_in, layout, allowed):
    scaling = 1.0 / math.sqrt(query_in.shape[-1])
    key_form = layout.replace("q", "k")
    scores = (
        jnp.einsum(
            layout + "," + key_form + "->bxhqk",
            query_in,
            key_in,
            preferred_element_type=jnp.float32,
        )
        * scaling
    )
    scores = jnp.where(allowed, scores, -1e30)
    highest = jnp.max(scores, axis=-1, keepdims=True)
    weight_sum = jnp.sum(jnp.exp(scores - highest), axis=-1, keepdims=True)
    log_total = highest + jnp.log(weight_sum)
    weights = jnp.where(allowed, jnp.exp(scores - log_total), 0.0)
    rounded = weights.astype(jnp.bfloat16)
    output = jnp.einsum(
        "bxhqk," + key_form + "->" + layout, rounded, value_in, preferred_element_type=jnp.float32
    ).astype(jnp.bfloat16)
    row_dots = jnp.einsum(
        layout + "," + layout + "->bxhq", grad_in, output, preferred_element_type=jnp.float32
    )
    dprobs = jnp.einsum(
        layout + "," + key_form + "->bxhqk", grad_in, value_in, preferred_element_type=jnp.float32
    )
    dscores = (weights * (dprobs - row_dots[..., None]) * scaling).astype(jnp.bfloat16)
    grad_query = jnp.einsum(
        "bxhqk," + key_form + "->" + layout, dscores, key_in, preferred_element_type=jnp.float32
    ).astype(jnp.bfloat16)
    grad_key = jnp.einsum(
        "bxhqk," + layout + "->" + key_form, dscores, query_in, preferred_element_type=jnp.float32
    )
    grad_value = jnp.einsum(
        "bxhqk," + layout + "->" + key_form, rounded, grad_in, preferred_element_type=jnp.float32
    )
    return (output, grad_query, grad_key, grad_value)


def merge_heads(first_part, second_part):
    stacked = jnp.stack((first_part, second_part), axis=4)
    shape = first_part.shape
    return stacked.reshape(shape[:3] + (2 * shape[3], shape[4]))


def per_device(queries, key_vecs, value_vecs, grad_out):
    arrays = (queries, key_vecs, value_vecs, grad_out)
    row_parts = tuple((array[:, :, :, 0::2] for array in arrays))
    col_parts = tuple((array[:, :, :, 1::2] for array in arrays))
    row_local = attend(
        row_parts[0], row_parts[1], row_parts[2], row_parts[3], "bxqhd", causal(queries.shape[2])
    )
    row_results = (
        row_local[0],
        row_local[1],
        row_local[2].astype(jnp.bfloat16),
        row_local[3].astype(jnp.bfloat16),
    )
    local_rows = col_parts[0].shape[1]
    gathered = (
        lax.all_gather(col_parts[1], "ctx", axis=1, tiled=True),
        lax.all_gather(col_parts[2], "ctx", axis=1, tiled=True),
    )
    query_rows = lax.axis_index("ctx") * local_rows + jnp.arange(local_rows)
    key_rows = jnp.arange(gathered[0].shape[1])
    allowed = key_rows[None, :] <= query_rows[:, None]
    col_local = attend(col_parts[0], gathered[0], gathered[1], col_parts[3], "bqxhd", allowed)
    summed = (
        lax.psum_scatter(col_local[2], "ctx", scatter_dimension=1, tiled=True),
        lax.psum_scatter(col_local[3], "ctx", scatter_dimension=1, tiled=True),
    )
    col_results = (
        col_local[0],
        col_local[1],
        summed[0].astype(jnp.bfloat16),
        summed[1].astype(jnp.bfloat16),
    )
    return (
        merge_heads(row_results[0], col_results[0]),
        merge_heads(row_results[1], col_results[1]),
        merge_heads(row_results[2], col_results[2]),
        merge_heads(row_results[3], col_results[3]),
    )


def solution(mesh):
    body = fused if mesh.shape["ctx"] == 4 else per_device
    placed = (
        P(("groups", "dp"), "ctx", None, "head", None),
        P(("groups", "dp"), "ctx", None, "head", None),
        P(("groups", "dp"), "ctx", None, "head", None),
        P(("groups", "dp"), "ctx", None, "head", None),
    )
    return jax.shard_map(
        body,
        mesh=mesh,
        in_specs=placed,
        out_specs=(
            P(("groups", "dp"), "ctx", None, "head", None),
            P(("groups", "dp"), "ctx", None, "head", None),
            P(("groups", "dp"), "ctx", None, "head", None),
            P(("groups", "dp"), "ctx", None, "head", None),
        ),
        check_vma=False,
    )
```
